128 devices in a mesh: row: 8 (over z_hi, y), col: 16 (over x, z_lo, core).
Axes of the slice: x: 4, y: 4, z: 4 (z_hi: 2, z_lo: 2; z = z_hi * 2 + z_lo), core: 2. Of those that a mesh axis runs over, the one named last changes fastest.
Arguments:
- positions: float32 [3, 16384], P(None, ('row', 'col')), may hold values from 0 to 5
- species: int32 [16384], P(('row', 'col')), may hold values from 0 to 99
- tile_list: int32 [8, 16, 2, 3], P('row', 'col'), may hold values from 0 to 15, as said below
- pair_mask: int32 [8, 16, 2, 128, 128], P('row', 'col'), may hold values 0 or 1
- embed: float32 [100, 128], replicated, may hold values from -6 to 6
- w_in: float32 [2, 128, 128], replicated, may hold values from -0.5 to 0.5
- rbf_weight: bfloat16 [2, 256, 128], replicated, may hold values from -1 to 1
- rbf_bias: float32 [2, 128], replicated, may hold values from -4 to 4
- filt_weight: bfloat16 [2, 128, 128], replicated, may hold values from -1 to 1
- w_update1: float32 [2, 128, 128], replicated, may hold values from -1 to 1
- w_update2: float32 [2, 128, 128], replicated, may hold values from -0.5 to 0.5
- w_out1: float32 [128, 64], replicated, may hold values from -0.5 to 0.5
- w_out2: float32 [64], replicated, may hold values from -0.75 to 0.75
Outputs:
- atom_energy: float32 [16384], P(('row', 'col'))
- forces: float32 [3, 16384], P(None, ('row', 'col'))
The draws below stay inside these ranges and needn't reach their ends.
Inputs may be any that keep to these rules, and one draw needn't show every extreme that they name: `tile_list`: A live slot (flag 1) names a row block below 16 and a column block below 8; the live slots of one device name distinct row blocks and come first; a dead slot is all zeros; every device has at least one live slot and some device has all 2.
All inputs are finite; a program needn't handle non-finite values. No bound on the sum of `pair_mask` on one device may be relied on, other than what follows from the above.
Results may differ from the reference program's by a relative error of at most 0.007.
Values sent between devices are 32-bit elements; how exact they have to be, the bound alone decides.
No kernel may reach another device: no remote copies, remote signals or barrier semaphores. Data moves between devices by JAX's collectives and lax.ppermute only.
A program may use at most 192 MiB of HBM per device.

```python
import math
import jax
import jax.numpy as jnp
from jax import lax

BLK = 128
FILTERS = 128
GAUSS = 256
SPECIES = 100
HALF = 64
LAYERS = 2
KMAX = 2
NATOM = 16384
N_ROW = 8
N_COL = 16


def draw_tile_list(key, part):
    key_order, key_col, key_count, key_pick = jax.random.split(key, 4)
    devices_all = N_ROW * N_COL
    scores = jax.random.randint(key_order, (devices_all, N_COL), 0, 1 << 20) * N_COL + jnp.arange(N_COL, dtype=jnp.int32)[None, :]
    order = jnp.argsort(scores, axis=1)[:, :KMAX].astype(jnp.int32)
    col_pick = jax.random.randint(key_col, (devices_all, KMAX), 0, N_ROW).astype(jnp.int32)
    counts = jax.random.randint(key_count, (devices_all,), 1, KMAX + 1).astype(jnp.int32)
    chosen = jax.random.randint(key_pick, (), 0, devices_all)
    counts = jnp.where(jnp.arange(devices_all, dtype=jnp.int32) == chosen, KMAX, counts)
    live = (jnp.arange(KMAX, dtype=jnp.int32)[None, :] < counts[:, None]).astype(jnp.int32)
    table = jnp.stack([order * live, col_pick * live, live], axis=-1)
    return table.reshape(N_ROW, N_COL, KMAX, 3)


def plant(result, key, smallest, high):
    dims = result.shape
    place = [jax.random.randint(jax.random.fold_in(key, axis), (), 0, dims[axis]) for axis in range(len(dims))]
    result = result.at[tuple(place)].set(smallest)
    longest = dims.index(max(dims))
    place[longest] = (place[longest] + 1) % dims[longest]
    return result.at[tuple(place)].set(high)


def steps_of(stream_key, dims, shards, least, high):
    gain = 1.0
    for axis_at, shards_of in shards:
        draws = jax.random.uniform(jax.random.fold_in(jax.random.fold_in(stream_key, 6), axis_at), (shards_of,), jnp.float32, least / len(shards), high / len(shards))
        gain = gain * jnp.repeat(jnp.exp(draws), dims[axis_at] // shards_of).reshape((-1,) + (1,) * (len(dims) - 1 - axis_at))
    return gain


def scatter_about(key, dims, width, most, kind=jnp.bfloat16):
    values = jax.random.normal(key, dims, jnp.float32) * width
    return jnp.minimum(jnp.maximum(values, -most), most).astype(kind)


def setup_inputs(seed: int = 0) -> dict:
    key_list = jax.random.split(jax.random.key(seed), 14)
    positions = jnp.clip(5.0 * jax.random.uniform(key_list[0], (3, NATOM), jnp.float32) ** steps_of(key_list[0], (3, NATOM), ((1, 128),), -0.2, 0.2), 0.0, 5.0)
    species = plant(jax.random.randint(key_list[1], (NATOM,), 0, SPECIES), jax.random.fold_in(key_list[1], 1), 0, SPECIES - 1).astype(jnp.int32)
    tile_list = draw_tile_list(jax.random.fold_in(key_list[13], 71), 0)
    pair_mask = plant((jax.random.randint(key_list[3], (N_ROW, N_COL, KMAX, BLK, BLK), 0, 2) < 1).astype(jnp.int32), jax.random.fold_in(key_list[3], 1), 0, 1)
    embed = scatter_about(key_list[4], (SPECIES, FILTERS), 1.0, 6.0, jnp.float32)
    w_in = scatter_about(key_list[5], (LAYERS, FILTERS, FILTERS), FILTERS ** -0.5, 0.5, jnp.float32)
    rbf_weight = scatter_about(key_list[6], (LAYERS, GAUSS, FILTERS), (GAUSS // 8) ** -0.5, 1.0)
    rbf_bias = scatter_about(key_list[7], (LAYERS, FILTERS), 0.7, 4.0, jnp.float32)
    filt_weight = scatter_about(key_list[8], (LAYERS, FILTERS, FILTERS), (FILTERS // 4) ** -0.5, 1.0)
    w_update1 = scatter_about(key_list[9], (LAYERS, FILTERS, FILTERS), (FILTERS // 4) ** -0.5, 1.0, jnp.float32)
    w_update2 = scatter_about(key_list[10], (LAYERS, FILTERS, FILTERS), FILTERS ** -0.5, 0.5, jnp.float32)
    w_out1 = scatter_about(key_list[11], (FILTERS, HALF), FILTERS ** -0.5, 0.5, jnp.float32)
    w_out2 = scatter_about(key_list[12], (HALF,), HALF ** -0.5, 0.75, jnp.float32)
    return {"positions": positions, "species": species, "tile_list": tile_list, "pair_mask": pair_mask, "embed": embed, "w_in": w_in, "rbf_weight": rbf_weight, "rbf_bias": rbf_bias, "filt_weight": filt_weight, "w_update1": w_update1, "w_update2": w_update2, "w_out1": w_out1, "w_out2": w_out2}


CUTOFF = 5.0
NORM_DIV = 4.0
HIGH = lax.Precision.HIGHEST

def shifted_softplus(values):
    return jax.nn.softplus(values) - math.log(2.0)

def tile_message(row_coord, col_coord, col_feat, pair_gate, rbf_w, rbf_b, filt_w):
    offset = row_coord[:, :, None] - col_coord[:, None, :]
    distance = jnp.sqrt(lax.optimization_barrier(jnp.sum(offset * offset, axis=0)) + 0.01)
    n_gauss = rbf_w.shape[0]
    rows_here = distance.shape[0]
    feat_width = filt_w.shape[1]
    centers = jnp.arange(n_gauss).astype(distance.dtype) * (CUTOFF / n_gauss)
    sharpness = (n_gauss / CUTOFF) ** 2 / 32.0
    expand = jnp.exp(-sharpness * (distance[:, :, None] - centers) ** 2).astype(jnp.bfloat16)
    pre_act = jnp.dot(expand.reshape(rows_here * rows_here, n_gauss), rbf_w, preferred_element_type=jnp.float32) + rbf_b
    hidden = shifted_softplus(pre_act).astype(jnp.bfloat16)
    filters = jnp.dot(hidden, filt_w, preferred_element_type=jnp.float32).reshape(rows_here, rows_here, feat_width)
    envelope = jnp.where(distance < CUTOFF, 0.5 * (jnp.cos(math.pi * distance / CUTOFF) + 1.0), 0.0)
    envelope = envelope * pair_gate.astype(distance.dtype)
    return jnp.einsum('ijf,ij,jf->if', filters, envelope, col_feat) / NORM_DIV

def atom_update(message, w_one, w_two):
    return jnp.dot(shifted_softplus(jnp.dot(message, w_one, precision=HIGH)), w_two, precision=HIGH)

def energy_head(features, w_out1, w_out2):
    return jnp.dot(shifted_softplus(jnp.dot(features, w_out1, precision=HIGH)), w_out2, precision=HIGH)

def energy_parts(positions, species, tile_list, pair_mask, embed, w_in, rbf_weight, rbf_bias, filt_weight, w_update1, w_update2, w_out1, w_out2):
    n_blocks = N_ROW * N_COL
    onehot = (species[:, None] == jnp.arange(SPECIES, dtype=jnp.int32)[None, :]).astype(embed.dtype)
    features = jnp.dot(onehot, embed, precision=HIGH)
    table = tile_list.reshape(N_ROW * N_COL * KMAX, 3)
    flat_idx = jnp.arange(N_ROW * N_COL * KMAX, dtype=jnp.int32)
    row_dev = flat_idx // (N_COL * KMAX)
    col_dev = flat_idx // KMAX % N_COL
    row_block = row_dev * N_COL + table[:, 0]
    col_block = table[:, 1] * N_COL + col_dev
    gates = pair_mask.reshape(N_ROW * N_COL * KMAX, BLK, BLK) * table[:, 2][:, None, None]
    block_pos = jnp.transpose(positions.reshape(3, n_blocks, BLK), (1, 0, 2))
    row_coord = block_pos[row_block]
    col_coord = block_pos[col_block]
    for layer_idx in range(LAYERS):
        mixed_in = jnp.dot(features, w_in[layer_idx], precision=HIGH)
        block_feat = mixed_in.reshape(n_blocks, BLK, FILTERS)
        rbf_w = rbf_weight[layer_idx]
        rbf_b = rbf_bias[layer_idx]
        filt_w = filt_weight[layer_idx]

        def one_tile(operands, rbf_w=rbf_w, rbf_b=rbf_b, filt_w=filt_w):
            return tile_message(operands[0], operands[1], operands[2], operands[3], rbf_w, rbf_b, filt_w)
        msgs = lax.map(jax.checkpoint(one_tile), (row_coord, col_coord, block_feat[col_block], gates))
        message = jnp.zeros((n_blocks, BLK, FILTERS), features.dtype).at[row_block].add(msgs)
        message = message.reshape(n_blocks * BLK, FILTERS)
        features = features + atom_update(message, w_update1[layer_idx], w_update2[layer_idx])
    return energy_head(features, w_out1, w_out2)

def reference(positions, species, tile_list, pair_mask, embed, w_in, rbf_weight, rbf_bias, filt_weight, w_update1, w_update2, w_out1, w_out2):

    def total_fn(coords):
        return energy_parts(coords, species, tile_list, pair_mask, embed, w_in, rbf_weight, rbf_bias, filt_weight, w_update1, w_update2, w_out1, w_out2)
    energies, pull_back = jax.vjp(total_fn, positions)
    grads = pull_back(jnp.ones_like(energies))[0]
    return (energies, -grads)
```

```python
import math

import jax
import jax.numpy as jnp
from jax import lax
from jax.experimental import pallas as pl
from jax.experimental.pallas import tpu as pltpu
from jax.sharding import PartitionSpec as P

BLK = 128
GAUSS = 256
CUTOFF = 5.0
NORM_DIV = 4.0
STEP = CUTOFF / GAUSS
LN2 = math.log(2.0)
LOG2E = 1.0 / LN2
ALPHA = math.sqrt(LOG2E / 32.0)
SLOPE = -2.0 * LN2 * ALPHA / STEP
HIGH = lax.Precision.HIGHEST
GRP = 8
PIECES = ((0, 0), (0, 1), (1, 0), (1, 1))
HALF_ROWS = 64

T_ROW, T_COL, T_LIVE = 0, 2, 4
T_RSC, T_RSR = 6, 14
T_AGC, T_AGCS, T_AGR, T_AGRS = 18, 20, 22, 24
T_WROW, T_WCOL = 26, 58


SMEM = pl.BlockSpec(memory_space=pltpu.SMEM)
VMEM = pl.BlockSpec(memory_space=pltpu.VMEM)


def sds(*shape, dtype=jnp.float32):
    return jax.ShapeDtypeStruct(shape, dtype)


def hdot(a, b):
    return jnp.dot(a, b, precision=HIGH, preferred_element_type=jnp.float32)


def hdot_t(a, b):
    return lax.dot_general(
        a, b, (((1,), (1,)), ((), ())), precision=HIGH, preferred_element_type=jnp.float32
    )


def ssp_sig(v):
    e = jnp.exp(-jnp.abs(v))
    act = jnp.maximum(v, 0.0) + jnp.log(1.0 + e) - LN2
    sig = jnp.where(v >= 0.0, 1.0, e) / (1.0 + e)
    return act, sig


def feature_rows(tile, embed):
    spec = jnp.transpose(tile)[:, 3:4]
    kinds = lax.broadcasted_iota(jnp.int32, (BLK, BLK), 1).astype(jnp.float32)
    onehot = jnp.where(spec == kinds, 1.0, 0.0)
    return hdot(onehot, embed)


def spread(mat, base, width):
    turned = pltpu.roll(mat, lax.rem(BLK - base, BLK), axis=1)
    return jnp.concatenate(
        [jnp.broadcast_to(turned[:, k : k + 1], (BLK, width)) for k in range(GRP)], axis=0
    )


def basis(xmat, base):
    ticks = lax.broadcasted_iota(jnp.int32, (1, GAUSS), 1).astype(jnp.float32) * ALPHA
    u = spread(xmat, base, GAUSS) - ticks
    return u, jnp.exp2(-(u * u))


def geo_body(tab, c16, r8, mask, embed, w_in, x_o, c_o, dc_o, feat_o):
    for s in range(2):
        rt = c16[tab[T_ROW + s]]
        ct = r8[tab[T_COL + s]]
        ctt = jnp.transpose(ct)
        d2 = jnp.zeros((BLK, BLK), jnp.float32)
        for a in range(3):
            off = rt[a : a + 1, :] - ctt[:, a : a + 1]
            d2 = d2 + off * off
        d = jnp.sqrt(d2 + 0.01)
        live = (tab[T_LIVE + s]).astype(jnp.float32) / NORM_DIV
        gate = jnp.transpose(mask[s].astype(jnp.float32)) * live
        ang = d * (math.pi / CUTOFF)
        near = d < CUTOFF
        env = jnp.where(near, 0.5 * (jnp.cos(ang) + 1.0), 0.0) * gate
        denv = jnp.where(near, (-0.5 * math.pi / CUTOFF) * jnp.sin(ang), 0.0) * gate
        x_o[s] = d * (ALPHA / STEP)
        c_o[s] = env
        dc_o[s] = denv
        feat_o[s] = hdot(feature_rows(ct, embed[...]), w_in[...])


def geo_call(tab, c16, r8, mask, embed, w_in):
    return pl.pallas_call(
        geo_body,
        out_shape=[sds(2, BLK, BLK)] * 4,
        in_specs=[SMEM] + [VMEM] * 5,
        out_specs=[VMEM] * 4,
        name="geo",
    )(tab, c16, r8, mask, embed, w_in)


def msg0_body(xm, cm, feat, w, b, f, m_o):
    def step(it, _):
        s = it // (BLK // GRP)
        base = pl.multiple_of(lax.rem(it, BLK // GRP) * GRP, GRP)
        _, ex = basis(xm[s], base)
        pre = jnp.dot(ex.astype(jnp.bfloat16), w[...], preferred_element_type=jnp.float32) + b[...]
        hid = jnp.log2(1.0 + jnp.exp2(pre * LOG2E)) - 1.0
        fil = jnp.dot(hid.astype(jnp.bfloat16), f[...], preferred_element_type=jnp.float32)
        fil = fil * spread(cm[s] * LN2, base, BLK)
        feats = feat[s]
        rows = [
            jnp.sum(fil[k * BLK : (k + 1) * BLK] * feats, axis=0, keepdims=True) for k in range(GRP)
        ]
        m_o[s, pl.ds(base, GRP), :] = jnp.concatenate(rows, axis=0)
        return 0

    lax.fori_loop(0, 2 * BLK // GRP, step, 0)


def msg0_call(xm, cm, feat, w, b, f):
    return pl.pallas_call(
        msg0_body,
        out_shape=sds(2, BLK, BLK),
        in_specs=[VMEM] * 6,
        out_specs=VMEM,
        name="msg0",
    )(xm, cm, feat, w, b, f)


def fil1_body(xm, cm, w, b, f, o, *, half):
    base = half * HALF_ROWS + pl.program_id(0) * GRP
    _, ex = basis(xm[...], base)
    pre = jnp.dot(ex.astype(jnp.bfloat16), w[...], preferred_element_type=jnp.float32) + b[...]
    hid = jnp.log2(1.0 + jnp.exp2(pre * LOG2E)) - 1.0
    fil = jnp.dot(hid.astype(jnp.bfloat16), f[...], preferred_element_type=jnp.float32)
    fil = fil * spread(cm[...] * LN2, base, BLK)
    o[...] = fil.astype(jnp.bfloat16).reshape(GRP, BLK, BLK)


def const_spec(*shape):
    zeros = (0,) * len(shape)
    return pl.BlockSpec(shape, lambda g: zeros)


def slot_spec(slot):
    return pl.BlockSpec((None, BLK, BLK), lambda g: (slot, 0, 0))


PIECE_SPEC = pl.BlockSpec((GRP, BLK, BLK), lambda g: (g, 0, 0))
PIECE = (HALF_ROWS, BLK, BLK)


def fil1_call(piece, xm, cm, w, b, f):
    slot, half = piece
    return pl.pallas_call(
        lambda *refs: fil1_body(*refs, half=half),
        grid=(HALF_ROWS // GRP,),
        out_shape=sds(*PIECE, dtype=jnp.bfloat16),
        in_specs=[
            slot_spec(slot),
            slot_spec(slot),
            const_spec(GAUSS, BLK),
            const_spec(1, BLK),
            const_spec(BLK, BLK),
        ],
        out_specs=PIECE_SPEC,
        name=f"fil1_{slot}{half}",
    )(xm, cm, w, b, f)


def tan_body(xm, cm, dcm, feat, w, b, f0, f1, o0, o1, *, half):
    base = half * HALF_ROWS + pl.program_id(0) * GRP
    u, ex = basis(xm[...], base)
    pre = jnp.dot(ex.astype(jnp.bfloat16), w[...], preferred_element_type=jnp.float32) + b[...]
    dpre = jnp.dot((u * ex).astype(jnp.bfloat16), w[...], preferred_element_type=jnp.float32)
    p2 = pre * LOG2E
    lg = jnp.log2(1.0 + jnp.exp2(p2))
    dhid = jnp.exp2(p2 - lg) * dpre
    cd = spread(cm[...] * SLOPE, base, 2 * BLK)
    ch = spread(dcm[...] * LN2, base, 2 * BLK)
    mix = (ch * (lg - 1.0) + cd * dhid).astype(jnp.bfloat16)
    t0 = jnp.dot(mix[:, :BLK], f0[...], preferred_element_type=jnp.float32)
    t1 = jnp.dot(mix[:, BLK:], f1[...], preferred_element_type=jnp.float32)
    o0[...] = (t0.reshape(GRP, BLK, BLK) * feat[...][None]).astype(jnp.bfloat16)
    o1[...] = t1.astype(jnp.bfloat16).reshape(GRP, BLK, BLK)


def tan_call(piece, xm, cm, dcm, feat, w, b, f0, f1):
    slot, half = piece
    return pl.pallas_call(
        lambda *refs: tan_body(*refs, half=half),
        grid=(HALF_ROWS // GRP,),
        out_shape=[sds(*PIECE, dtype=jnp.bfloat16)] * 2,
        in_specs=[
            slot_spec(slot),
            slot_spec(slot),
            slot_spec(slot),
            slot_spec(slot),
            const_spec(GAUSS, 2 * BLK),
            const_spec(1, 2 * BLK),
            const_spec(BLK, BLK),
            const_spec(BLK, BLK),
        ],
        out_specs=[PIECE_SPEC] * 2,
        name=f"tan_{slot}{half}",
    )(xm, cm, dcm, feat, w, b, f0, f1)


def pick(code, sources, store):
    for n, read in enumerate(sources):

        @pl.when(code == n)
        def _(read=read):
            store(read())


def readers(refs):
    out = []
    for ref in refs:
        if len(ref.shape) == 2:
            out.append(lambda ref=ref: ref[...])
        else:
            out.extend([lambda ref=ref, n=n: ref[n] for n in range(ref.shape[0])])
    return out


def select_body(tab, *refs, at):
    sources, o = readers(refs[:-1]), refs[-1]
    for s in range(2):

        def store(v, s=s):
            o[s] = v

        pick(tab[at + s], sources, store)


def select_call(tab, blocks, at, name):
    return pl.pallas_call(
        lambda *refs: select_body(*refs, at=at),
        out_shape=sds(2, BLK, BLK),
        in_specs=[SMEM] + [VMEM] * len(blocks),
        out_specs=VMEM,
        name=name,
    )(tab, *blocks)


def combine_body(tab, *refs, at):
    sources, outs = readers(refs[:-4]), refs[-4:]
    for o in outs:
        o[...] = jnp.zeros_like(o)
    for n, read in enumerate(sources):
        for k, o in enumerate(outs):

            @pl.when(tab[at + n] == k)
            def _(read=read, o=o):
                o[...] += read()


def combine_call(tab, blocks, at, name):
    return pl.pallas_call(
        lambda *refs: combine_body(*refs, at=at),
        out_shape=[sds(BLK, BLK)] * 4,
        in_specs=[SMEM] + [VMEM] * len(blocks),
        out_specs=[VMEM] * 4,
        name=name,
    )(tab, *blocks)


def resolve(tab, at, refs, scratch):
    sources = readers(refs)
    for s in range(2):

        def store(v, s=s):
            scratch[s] = v

        pick(tab[at + s], sources, store)


def msg1_body(tab, *refs, nsrc):
    src, pieces, o, feat_o = refs[:nsrc], refs[nsrc : nsrc + 4], refs[-2], refs[-1]
    g = pl.program_id(0)

    @pl.when(g == 0)
    def _():
        resolve(tab, T_AGR, src, feat_o)

    for (slot, half), piece in zip(PIECES, pieces):
        base = pl.multiple_of(half * HALF_ROWS + g * GRP, GRP)
        feats = feat_o[slot]
        rows = [
            jnp.sum(piece[k].astype(jnp.float32) * feats, axis=0, keepdims=True) for k in range(GRP)
        ]
        o[slot, pl.ds(base, GRP), :] = jnp.concatenate(rows, axis=0)


def whole(arr):
    return const_spec(*arr.shape)


def msg1_call(tab, blocks, pieces):
    return pl.pallas_call(
        lambda *refs: msg1_body(*refs, nsrc=len(blocks)),
        grid=(HALF_ROWS // GRP,),
        out_shape=[sds(2, BLK, BLK)] * 2,
        in_specs=[SMEM] + [whole(a) for a in blocks] + [PIECE_SPEC] * 4,
        out_specs=[const_spec(2, BLK, BLK)] * 2,
        name="msg1",
    )(tab, *blocks, *pieces)


def dfeat_body(tab, *refs, nsrc):
    src, pieces, o, grad_o = refs[:nsrc], refs[nsrc : nsrc + 4], refs[-2], refs[-1]
    g = pl.program_id(0)

    @pl.when(g == 0)
    def _():
        resolve(tab, T_AGC, src, grad_o)
        o[...] = jnp.zeros_like(o)

    for (slot, half), piece in zip(PIECES, pieces):
        base = pl.multiple_of(half * HALF_ROWS + g * GRP, GRP)
        rows = grad_o[slot, pl.ds(base, GRP), :]
        acc = o[slot]
        for k in range(GRP):
            acc = acc + piece[k].astype(jnp.float32) * rows[k : k + 1, :]
        o[slot] = acc


def dfeat_call(tab, blocks, pieces):
    return pl.pallas_call(
        lambda *refs: dfeat_body(*refs, nsrc=len(blocks)),
        grid=(HALF_ROWS // GRP,),
        out_shape=[sds(2, BLK, BLK)] * 2,
        in_specs=[SMEM] + [whole(a) for a in blocks] + [PIECE_SPEC] * 4,
        out_specs=[const_spec(2, BLK, BLK)] * 2,
        name="dfeat",
    )(tab, *blocks, *pieces)


def slope_step(g, pieces, grads, feats, o):
    lanes = lax.broadcasted_iota(jnp.int32, (BLK, BLK), 1)
    for (slot, half), piece in zip(PIECES, pieces):
        base = half * HALF_ROWS + g * GRP
        rows = piece[...]
        if feats is not None:
            rows = rows * feats[slot].astype(jnp.bfloat16)[None]
        prod = lax.dot_general(
            rows.reshape(GRP * BLK, BLK),
            grads[slot].astype(jnp.bfloat16),
            (((1,), (1,)), ((), ())),
            preferred_element_type=jnp.float32,
        )
        acc = o[slot]
        for k in range(GRP):
            acc = jnp.where(lanes == base + k, prod[k * BLK : (k + 1) * BLK], acc)
        o[slot] = acc


def slope1_body(grads, feats, *refs):
    pieces, o = refs[:4], refs[4]

    @pl.when(pl.program_id(0) == 0)
    def _():
        o[...] = jnp.zeros_like(o)

    slope_step(pl.program_id(0), pieces, grads, feats, o)


def slope1_call(grads, feats, pieces):
    return pl.pallas_call(
        slope1_body,
        grid=(HALF_ROWS // GRP,),
        out_shape=sds(2, BLK, BLK),
        in_specs=[whole(grads), whole(feats)] + [PIECE_SPEC] * 4,
        out_specs=const_spec(2, BLK, BLK),
        name="slope1",
    )(grads, feats, *pieces)


def force_body(tab, c16, r8, xm, first, *refs, nsrc):
    src, pieces, rf_o, cf_o, grad_s, acc_s = (
        refs[:nsrc],
        refs[nsrc : nsrc + 4],
        refs[-4],
        refs[-3],
        refs[-2],
        refs[-1],
    )
    g = pl.program_id(0)

    @pl.when(g == 0)
    def _():
        resolve(tab, T_AGC, src, grad_s)
        acc_s[...] = jnp.zeros_like(acc_s)

    slope_step(g, pieces, grad_s, None, acc_s)

    @pl.when(g == pl.num_programs(0) - 1)
    def _():
        for s in range(2):
            rt = c16[tab[T_ROW + s]]
            ctt = jnp.transpose(r8[tab[T_COL + s]])
            pull = -(first[s] + acc_s[s]) / (xm[s] * (STEP / ALPHA))
            rows, cols = [], []
            for a in range(3):
                comp = pull * (rt[a : a + 1, :] - ctt[:, a : a + 1])
                rows.append(jnp.sum(comp, axis=0, keepdims=True))
                cols.append(jnp.sum(comp, axis=1, keepdims=True))
            rf_o[s] = jnp.concatenate(rows + [jnp.zeros((5, BLK), jnp.float32)], axis=0)
            cols = jnp.concatenate(cols + [jnp.zeros((BLK, BLK - 3), jnp.float32)], axis=1)
            cf_o[s] = -jnp.transpose(cols)[:8]


def force_call(tab, c16, r8, xm, first, blocks, pieces):
    return pl.pallas_call(
        lambda *refs: force_body(*refs, nsrc=len(blocks)),
        grid=(HALF_ROWS // GRP,),
        out_shape=[sds(2, 8, BLK)] * 2,
        in_specs=[SMEM]
        + [whole(a) for a in (c16, r8, xm, first)]
        + [whole(a) for a in blocks]
        + [PIECE_SPEC] * 4,
        out_specs=[const_spec(2, 8, BLK)] * 2,
        scratch_shapes=[pltpu.VMEM((2, BLK, BLK), jnp.float32)] * 2,
        name="force",
    )(tab, c16, r8, xm, first, *blocks, *pieces)


def sum_body(tab, rows, cols, o):
    acc = jnp.zeros((8, BLK), jnp.float32)
    for n in range(rows.shape[0]):
        acc = acc + rows[n] * tab[T_WROW + n].astype(jnp.float32)
    for n in range(cols.shape[0]):
        acc = acc + cols[n] * tab[T_WCOL + n].astype(jnp.float32)
    o[...] = acc[:3]


def sum_call(tab, rows, cols):
    return pl.pallas_call(
        sum_body,
        out_shape=sds(3, BLK),
        in_specs=[SMEM, VMEM, VMEM],
        out_specs=VMEM,
        name="sum_forces",
    )(tab, rows, cols)


def up1_body(m0, m1, m2, m3, tile, embed, w1, w2, w_in, feat_o, sig_o, mixed_o):
    message = (m0[...] + m1[...]) + (m2[...] + m3[...])
    act, sig = ssp_sig(hdot(message, w1[...]))
    feats = feature_rows(tile[...], embed[...]) + hdot(act, w2[...])
    feat_o[...] = feats
    sig_o[...] = sig
    mixed_o[...] = hdot(feats, w_in[...])


def up2_body(m0, m1, m2, m3, feat, w1, w2, wo1, wo2, en_o, gfeat_o, gmsg_o):
    message = (m0[...] + m1[...]) + (m2[...] + m3[...])
    act, sig = ssp_sig(hdot(message, w1[...]))
    feats = feat[...] + hdot(act, w2[...])
    head, head_sig = ssp_sig(hdot(feats, wo1[...]))
    en_o[...] = hdot_t(jnp.broadcast_to(wo2[...], (8, wo2.shape[1])), head)[:1]
    gfeat = hdot_t(head_sig * wo2[...], wo1[...])
    gfeat_o[...] = gfeat
    gmsg_o[...] = hdot_t(hdot_t(gfeat, w2[...]) * sig, w1[...])


def up3_body(m0, m1, m2, m3, gfeat, sig, w_in, w1, w2, gmsg_o):
    total = (m0[...] + m1[...]) + (m2[...] + m3[...])
    gf = gfeat[...] + hdot_t(total, w_in[...])
    gmsg_o[...] = hdot_t(hdot_t(gf, w2[...]) * sig[...], w1[...])


def plain_call(fn, outs, args, name):
    return pl.pallas_call(
        fn, out_shape=outs, in_specs=[VMEM] * len(args), out_specs=[VMEM] * len(outs), name=name
    )(*args)


X_SHIFT = {k: [(i, ((i // 4 + k) % 4) * 4 + i % 4) for i in range(16)] for k in (1, 2, 3)}
Y_SHIFT = {k: [(i, (i // 4) * 4 + (i + k) % 4) for i in range(8)] for k in (1, 2, 3)}
CORE = [(i, i ^ 1) for i in range(16)]
Z_LO = [(i, i ^ 2) for i in range(16)]
Z_HI = [(i, i ^ 4) for i in range(8)]


def by_x(v):
    return [lax.ppermute(v, "col", X_SHIFT[k]) for k in (1, 2, 3)]


def by_y(v):
    return [lax.ppermute(v, "row", Y_SHIFT[k]) for k in (1, 2, 3)]


def core(v):
    return lax.ppermute(v, "col", CORE)


def z_lo(v):
    return lax.ppermute(v, "col", Z_LO)


def z_hi(v):
    return lax.ppermute(v, "row", Z_HI)


def index_table(lists_c, lists_r):
    q, r = lax.axis_index("col"), lax.axis_index("row")
    mx, mzl, mco = q // 4, (q // 2) % 2, q % 2
    mz, my = r // 4, r % 4
    order = jnp.array([0, 2, 1, 3])
    own = lists_c[0]
    a, b, live = own[:, 0], own[:, 1], own[:, 2]

    def ax(t):
        return t // 4, (t // 2) % 2, t % 2

    tx, tz, tc = ax(a)
    row_idx = ((mx - tx) % 4) * 4 + (tz ^ mzl) * 2 + (tc ^ mco)
    col_idx = ((my - b % 4) % 4) * 2 + ((b // 4) ^ mz)
    agc = jnp.where(tz == mzl, (mx - tx) % 4 + 4 * (tc ^ mco), 8 + jnp.arange(2))
    agr = jnp.where(b // 4 == mz, (my - b % 4) % 4, 4 + jnp.arange(2))
    cand = lists_c.reshape(4, 4, 2, 3)[:, order]
    near = cand[0].reshape(8, 3)
    nx, nz, nc = ax(near[:, 0])
    rsc = jnp.where((near[:, 2] == 1) & (nz == mzl) & (nc == mco), (nx - mx) % 4, -1)
    nearr = lists_r[:2].reshape(4, 3)
    rsr = jnp.where(
        (nearr[:, 2] == 1) & (nearr[:, 1] // 4 == mz), (nearr[:, 1] % 4 - my) % 4, -1
    )
    px, pz, pc = ax(lists_c[2][:, 0])
    agcs = jnp.where(pz == mzl, (mx - px) % 4 + 4 * (pc ^ mco), 0)
    pb = lists_r[1][:, 1]
    agrs = jnp.where(pb // 4 == mz, (my - pb % 4) % 4, 0)
    flat_c = cand.reshape(32, 3)
    wrow = (flat_c[:, 2] == 1) & (flat_c[:, 0] == q)
    flat_r = lists_r.reshape(16, 3)
    wcol = (flat_r[:, 2] == 1) & (flat_r[:, 1] == r)
    parts = [row_idx, col_idx, live, rsc, rsr, agc, agcs, agr, agrs, wrow, wcol]
    return jnp.concatenate([p.astype(jnp.int32) for p in parts])


def body(
    positions,
    species,
    tile_list,
    pair_mask,
    embed,
    w_in,
    rbf_weight,
    rbf_bias,
    filt_weight,
    w_update1,
    w_update2,
    w_out1,
    w_out2,
):
    f32 = jnp.float32
    lists = jnp.pad(tile_list.reshape(1, 6).astype(f32), ((0, 0), (0, BLK - 6)))
    tile = jnp.concatenate(
        [positions, species.astype(f32)[None], lists, jnp.zeros((3, BLK), f32)], axis=0
    )
    c2 = jnp.stack([tile, core(tile)])
    c4 = jnp.concatenate([c2, z_lo(c2)])
    c16 = jnp.concatenate([c4] + by_x(c4))
    r2 = jnp.stack([tile, z_hi(tile)])
    r8 = jnp.concatenate([r2] + by_y(r2))
    lists_c = c16[:, 4, :6].astype(jnp.int32).reshape(16, 2, 3)
    lists_r = r8[:, 4, :6].astype(jnp.int32).reshape(8, 2, 3)
    tab = index_table(lists_c, lists_r)
    embed_p = jnp.pad(embed, ((0, BLK - embed.shape[0]), (0, 0)))
    masks = pair_mask.reshape(2, BLK, BLK)
    b0, b1 = rbf_bias[0][None], rbf_bias[1][None]
    w_both = jnp.concatenate([rbf_weight[0], rbf_weight[1]], axis=1)
    b_both = jnp.concatenate([b0, b1], axis=1)
    wo2 = w_out2[None]

    xm, cm, dcm, feat0 = geo_call(tab, c16, r8, masks, embed_p, w_in[0])

    def gather_rows(v):
        four = [v] + by_x(v)
        return four, core(jnp.stack(four))

    def reduce_rows(m, name):
        far = z_lo(m)
        both = core(m)
        rest = core(far)
        parts = combine_call(tab, [m, far, both, rest], T_RSC, name)
        return [parts[0]] + [lax.ppermute(parts[k], "col", X_SHIFT[k]) for k in (1, 2, 3)]

    m0 = msg0_call(xm, cm, feat0, rbf_weight[0], b0, filt_weight[0])
    fil1 = [fil1_call(p, xm, cm, rbf_weight[1], b1, filt_weight[1]) for p in PIECES]
    tans = [
        tan_call(p, xm, cm, dcm, feat0, w_both, b_both, filt_weight[0], filt_weight[1])
        for p in PIECES
    ]
    parts = reduce_rows(m0, "combine0")
    own_feat, sig0, mixed1 = plain_call(
        up1_body,
        [sds(BLK, BLK)] * 3,
        [*parts, tile, embed_p, w_update1[0], w_update2[0], w_in[1]],
        "update0",
    )
    four = [mixed1] + by_y(mixed1)
    sent = z_hi(select_call(tab, four, T_AGRS, "select_x"))
    m1, feat1 = msg1_call(tab, [*four, sent], fil1)
    parts = reduce_rows(m1, "combine1")
    energy, gfeat2, gmsg1 = plain_call(
        up2_body,
        [sds(1, BLK), sds(BLK, BLK), sds(BLK, BLK)],
        [*parts, own_feat, w_update1[1], w_update2[1], w_out1, wo2],
        "update1",
    )
    four, other = gather_rows(gmsg1)
    sent = z_lo(select_call(tab, [*four, other], T_AGCS, "select_g1"))
    dfeat, grad1 = dfeat_call(tab, [*four, other, sent], fil1)
    slope1 = slope1_call(grad1, feat1, [t[1] for t in tans])
    far = z_hi(dfeat)
    parts = combine_call(tab, [dfeat, far], T_RSR, "combine_d")
    parts = [parts[0]] + [lax.ppermute(parts[k], "row", Y_SHIFT[k]) for k in (1, 2, 3)]
    (gmsg0,) = plain_call(
        up3_body,
        [sds(BLK, BLK)],
        [*parts, gfeat2, sig0, w_in[1], w_update1[0], w_update2[0]],
        "update2",
    )
    four, other = gather_rows(gmsg0)
    sent = z_lo(select_call(tab, [*four, other], T_AGCS, "select_g0"))
    rf, cf = force_call(
        tab, c16, r8, xm, slope1, [*four, other, sent], [t[0] for t in tans]
    )
    rf4 = jnp.concatenate([rf, z_lo(rf)])
    rf8 = jnp.concatenate([rf4, core(rf4)])
    rf32 = jnp.concatenate([rf8] + by_x(rf8))
    cf4 = jnp.concatenate([cf, z_hi(cf)])
    cf16 = jnp.concatenate([cf4] + by_y(cf4))
    forces = sum_call(tab, rf32, cf16)
    return (energy.reshape(BLK), forces)


def solution(mesh):
    return jax.shard_map(
        body,
        mesh=mesh,
        in_specs=(
            P(None, ("row", "col")),
            P(("row", "col")),
            P("row", "col", None, None),
            P("row", "col", None, None, None),
            P(),
            P(),
            P(),
            P(),
            P(),
            P(),
            P(),
            P(),
            P(),
        ),
        out_specs=(P(("row", "col")), P(None, ("row", "col"))),
        check_vma=False,
    )
```

```python
import math

import jax
import jax.numpy as jnp
from jax import lax
from jax.experimental import pallas as pl
from jax.experimental.pallas import tpu as pltpu
from jax.sharding import PartitionSpec as P

BLK = 128
GAUSS = 256
CUTOFF = 5.0
NORM_DIV = 4.0
STEP = CUTOFF / GAUSS
LN2 = math.log(2.0)
LOG2E = 1.0 / LN2
ALPHA = math.sqrt(LOG2E / 32.0)
SLOPE = -2.0 * LN2 * ALPHA / STEP
HIGH = lax.Precision.HIGHEST
GRP = 8
SUB = 4

T_ROW, T_COL, T_LIVE = 0, 2, 4
T_RSC, T_RSR = 6, 14
T_AGC, T_AGCS, T_AGR, T_AGRS = 18, 20, 22, 24
T_WROW, T_WCOL = 26, 58


SMEM = pl.BlockSpec(memory_space=pltpu.SMEM)
VMEM = pl.BlockSpec(memory_space=pltpu.VMEM)


def near(*shape, dtype=jnp.float32):
    return pltpu.VMEM(shape, dtype)


def call(fn, outs, tab, args, weights=(), scratch=(), name=None):
    args = [pltpu.with_memory_space_constraint(a, pltpu.VMEM) for a in args]
    tabs = [] if tab is None else [tab]
    return pl.pallas_call(
        fn,
        out_shape=list(outs),
        in_specs=[SMEM] * len(tabs) + [VMEM] * (len(args) + len(weights)),
        out_specs=[VMEM] * len(outs),
        scratch_shapes=list(scratch),
        compiler_params=pltpu.CompilerParams(vmem_limit_bytes=16 << 20),
        name=name,
    )(*tabs, *args, *weights)


def hdot(a, b):
    return jnp.dot(a, b, precision=HIGH, preferred_element_type=jnp.float32)


def hdot_t(a, b):
    return lax.dot_general(
        a, b, (((1,), (1,)), ((), ())), precision=HIGH, preferred_element_type=jnp.float32
    )


def ssp_sig(v):
    e = jnp.exp(-jnp.abs(v))
    act = jnp.maximum(v, 0.0) + jnp.log(1.0 + e) - LN2
    sig = jnp.where(v >= 0.0, 1.0, e) / (1.0 + e)
    return act, sig


def feature_rows(tile, embed):
    spec = jnp.transpose(tile)[:, 3:4]
    kinds = lax.broadcasted_iota(jnp.int32, (BLK, embed.shape[0]), 1).astype(jnp.float32)
    onehot = jnp.where(spec == kinds, 1.0, 0.0)
    return hdot(onehot, embed)


def turn(mat, base):
    return pltpu.roll(mat, lax.rem(BLK - base, BLK), axis=1)


def spread(turned, ks, width):
    return jnp.concatenate(
        [jnp.broadcast_to(turned[:, k : k + 1], (BLK, width)) for k in ks], axis=0
    )


def filter_body(
    tab, c16, r8, mask, embed, w_in, w_rbf, b_rbf, w_fil, m_o, feat_o, x_o, fil_o, q0_o, q1_o,
    cm_s, dcm_s, w_s,
):
    for s in range(2):
        rt = c16[tab[T_ROW + s]]
        ct = r8[tab[T_COL + s]]
        ctt = jnp.transpose(ct)
        d2 = jnp.zeros((BLK, BLK), jnp.float32)
        for a in range(3):
            off = rt[a : a + 1, :] - ctt[:, a : a + 1]
            d2 = d2 + off * off
        d = jnp.sqrt(d2 + 0.01)
        live = (tab[T_LIVE + s]).astype(jnp.float32) * (LN2 / NORM_DIV)
        gate = jnp.transpose(mask[s].astype(jnp.float32)) * live
        ang = d * (math.pi / CUTOFF)
        near_by = d < CUTOFF
        x_o[s] = d * (ALPHA / STEP)
        cm_s[s] = jnp.where(near_by, 0.5 * (jnp.cos(ang) + 1.0), 0.0) * gate
        dcm_s[s] = jnp.where(near_by, (-0.5 * math.pi / CUTOFF) * jnp.sin(ang), 0.0) * gate
        feat_o[s] = hdot(feature_rows(ct, embed[...]), w_in[0])
    w_s[:, :BLK] = w_rbf[0]
    w_s[:, BLK:] = w_rbf[1]

    def step(it, _):
        s = it // (BLK // GRP)
        base = pl.multiple_of(lax.rem(it, BLK // GRP) * GRP, GRP)
        xt, ct, dt = turn(x_o[s], base), turn(cm_s[s], base), turn(dcm_s[s], base)
        feats = feat_o[s]
        ticks = lax.broadcasted_iota(jnp.int32, (1, GAUSS), 1).astype(jnp.float32) * ALPHA
        bias = jnp.concatenate([b_rbf[0:1], b_rbf[1:2]], axis=1)
        rows = []
        for first in range(0, GRP, SUB):
            ks = range(first, first + SUB)
            u = spread(xt, ks, GAUSS) - ticks
            ex = jnp.exp2(-(u * u))
            pre = jnp.dot(ex.astype(jnp.bfloat16), w_s[...], preferred_element_type=jnp.float32)
            dpre = jnp.dot(
                (u * ex).astype(jnp.bfloat16), w_s[...], preferred_element_type=jnp.float32
            )
            c = spread(ct, ks, BLK)
            cd = c * (SLOPE / LN2)
            dc = spread(dt, ks, BLK)
            for layer in range(2):
                cols = slice(layer * BLK, (layer + 1) * BLK)
                p2 = (pre[:, cols] + bias[:, cols]) * LOG2E
                lg = jnp.log2(1.0 + jnp.exp2(p2))
                hid = lg - 1.0
                mix = dc * hid + cd * (jnp.exp2(p2 - lg) * dpre[:, cols])
                both = jnp.concatenate([hid.astype(jnp.bfloat16), mix.astype(jnp.bfloat16)], axis=0)
                both = jnp.dot(both, w_fil[layer], preferred_element_type=jnp.float32)
                fil = both[: SUB * BLK] * c
                slope = both[SUB * BLK :]
                at = pl.ds(base + first, SUB)
                if layer == 0:
                    for k in range(SUB):
                        here = slice(k * BLK, (k + 1) * BLK)
                        rows.append(jnp.sum(fil[here] * feats, axis=0, keepdims=True))
                    slope = slope.reshape(SUB, BLK, BLK) * feats[None]
                    q0_o[s, at] = slope.astype(jnp.bfloat16)
                else:
                    fil_o[s, at] = fil.astype(jnp.bfloat16).reshape(SUB, BLK, BLK)
                    q1_o[s, at] = slope.astype(jnp.bfloat16).reshape(SUB, BLK, BLK)
        m_o[s, pl.ds(base, GRP), :] = jnp.concatenate(rows, axis=0)
        return 0

    lax.fori_loop(0, 2 * BLK // GRP, step, 0)


STORE = (2, BLK, BLK, BLK)


def filter_call(tab, c16, r8, mask, embed, w_in, w_rbf, b_rbf, w_fil):
    big = near(*STORE, dtype=jnp.bfloat16)
    return call(
        filter_body,
        [near(2, BLK, BLK)] * 3 + [big] * 3,
        tab,
        [c16, r8],
        [mask, embed, w_in, w_rbf, b_rbf, w_fil],
        [pltpu.VMEM((2, BLK, BLK), jnp.float32)] * 2 + [pltpu.VMEM((GAUSS, 2 * BLK), jnp.bfloat16)],
        name="filters",
    )


def pick(code, sources, store):
    for n, read in enumerate(sources):

        @pl.when(code == n)
        def _(read=read):
            store(read())


def readers(refs):
    out = []
    for ref in refs:
        if len(ref.shape) == 2:
            out.append(lambda ref=ref: ref[...])
        else:
            out.extend([lambda ref=ref, n=n: ref[n] for n in range(ref.shape[0])])
    return out


def select_body(tab, *refs, at):
    sources, o = readers(refs[:-1]), refs[-1]
    for s in range(2):

        def store(v, s=s):
            o[s] = v

        pick(tab[at + s], sources, store)


def select_call(tab, blocks, at, name):
    return call(
        lambda *refs: select_body(*refs, at=at), [near(2, BLK, BLK)], tab, blocks, name=name
    )[0]


def combine_body(tab, *refs, at):
    sources, outs = readers(refs[:-4]), refs[-4:]
    for o in outs:
        o[...] = jnp.zeros_like(o)
    for n, read in enumerate(sources):
        for k, o in enumerate(outs):

            @pl.when(tab[at + n] == k)
            def _(read=read, o=o):
                o[...] += read()


def combine_call(tab, blocks, at, name):
    return call(
        lambda *refs: combine_body(*refs, at=at), [near(BLK, BLK)] * 4, tab, blocks, name=name
    )


def resolve(tab, at, refs, scratch):
    sources = readers(refs)
    for s in range(2):

        def store(v, s=s):
            scratch[s] = v

        pick(tab[at + s], sources, store)


def loop(fn):
    lax.fori_loop(0, 2 * BLK // GRP, lambda it, c: (fn(it), 0)[1], 0)


def place(it):
    return it // (BLK // GRP), pl.multiple_of(lax.rem(it, BLK // GRP) * GRP, GRP)


def msg1_body(tab, *refs):
    src, fil, o, feat_o = refs[:-3], refs[-3], refs[-2], refs[-1]
    resolve(tab, T_AGR, src, feat_o)

    def step(it):
        s, base = place(it)
        feats = feat_o[s]
        rows = [
            jnp.sum(fil[s, base + k].astype(jnp.float32) * feats, axis=0, keepdims=True)
            for k in range(GRP)
        ]
        o[s, pl.ds(base, GRP), :] = jnp.concatenate(rows, axis=0)

    loop(step)


def dfeat_body(tab, *refs):
    src, fil, o, grad_o = refs[:-3], refs[-3], refs[-2], refs[-1]
    resolve(tab, T_AGC, src, grad_o)
    o[...] = jnp.zeros_like(o)

    def step(it):
        s, base = place(it)
        rows = grad_o[s, pl.ds(base, GRP), :]
        acc = o[s]
        for k in range(GRP):
            acc = acc + fil[s, base + k].astype(jnp.float32) * rows[k : k + 1, :]
        o[s] = acc

    loop(step)


def slope_step(it, store, grads, feats, o):
    s, base = place(it)
    lanes = lax.broadcasted_iota(jnp.int32, (BLK, BLK), 1)
    rows = store[s, pl.ds(base, GRP)]
    if feats is not None:
        rows = rows * feats[s].astype(jnp.bfloat16)[None]
    prod = lax.dot_general(
        rows.reshape(GRP * BLK, BLK),
        grads[s].astype(jnp.bfloat16),
        (((1,), (1,)), ((), ())),
        preferred_element_type=jnp.float32,
    )
    acc = o[s]
    for k in range(GRP):
        acc = acc + jnp.where(lanes == base + k, prod[k * BLK : (k + 1) * BLK], 0.0)
    o[s] = acc


def slope1_body(grads, feats, store, o):
    o[...] = jnp.zeros_like(o)
    loop(lambda it: slope_step(it, store, grads, feats, o))


def force_body(tab, c16, r8, xm, first, *refs):
    src, store, rf_o, cf_o, grad_s, acc_s = refs[:-5], *refs[-5:]
    resolve(tab, T_AGC, src, grad_s)
    acc_s[...] = first[...]
    loop(lambda it: slope_step(it, store, grad_s, None, acc_s))
    for s in range(2):
        rt = c16[tab[T_ROW + s]]
        ctt = jnp.transpose(r8[tab[T_COL + s]])
        pull = -acc_s[s] / (xm[s] * (STEP / ALPHA))
        rows, cols = [], []
        for a in range(3):
            comp = pull * (rt[a : a + 1, :] - ctt[:, a : a + 1])
            rows.append(jnp.sum(comp, axis=0, keepdims=True))
            cols.append(jnp.sum(comp, axis=1, keepdims=True))
        rf_o[s] = jnp.concatenate(rows + [jnp.zeros((5, BLK), jnp.float32)], axis=0)
        cols = jnp.concatenate(cols + [jnp.zeros((BLK, BLK - 3), jnp.float32)], axis=1)
        cf_o[s] = -jnp.transpose(cols)[:8]


def sum_body(tab, *refs):
    rows, cols, o = refs[:4], refs[4:8], refs[8]
    acc = jnp.zeros((8, BLK), jnp.float32)
    for n in range(32):
        acc = acc + rows[n // 8][n % 8] * tab[T_WROW + n].astype(jnp.float32)
    for n in range(16):
        acc = acc + cols[n // 4][n % 4] * tab[T_WCOL + n].astype(jnp.float32)
    o[...] = acc[:3]


def sum_call(tab, rows, cols):
    args = [pltpu.with_memory_space_constraint(a, pltpu.VMEM) for a in (*rows, *cols)]
    return pl.pallas_call(
        sum_body,
        out_shape=jax.ShapeDtypeStruct((3, BLK), jnp.float32),
        in_specs=[SMEM] + [VMEM] * 8,
        out_specs=VMEM,
        name="sum_forces",
    )(tab, *args)


def up1_body(m0, m1, m2, m3, tile, embed, w1, w2, w_in, feat_o, sig_o, mixed_o):
    message = (m0[...] + m1[...]) + (m2[...] + m3[...])
    act, sig = ssp_sig(hdot(message, w1[0]))
    feats = feature_rows(tile[...], embed[...]) + hdot(act, w2[0])
    feat_o[...] = feats
    sig_o[...] = sig
    mixed_o[...] = hdot(feats, w_in[1])


def up2_body(m0, m1, m2, m3, feat, w1, w2, wo1, wo2, en_o, gfeat_o, gmsg_o):
    message = (m0[...] + m1[...]) + (m2[...] + m3[...])
    act, sig = ssp_sig(hdot(message, w1[1]))
    feats = feat[...] + hdot(act, w2[1])
    head, head_sig = ssp_sig(hdot(feats, wo1[...]))
    en_o[...] = hdot_t(jnp.broadcast_to(wo2[...], (8, wo2.shape[1])), head)[:1]
    gfeat = hdot_t(head_sig * wo2[...], wo1[...])
    gfeat_o[...] = gfeat
    gmsg_o[...] = hdot_t(hdot_t(gfeat, w2[1]) * sig, w1[1])


def up3_body(m0, m1, m2, m3, gfeat, sig, w_in, w1, w2, gmsg_o):
    total = (m0[...] + m1[...]) + (m2[...] + m3[...])
    gf = gfeat[...] + hdot_t(total, w_in[1])
    gmsg_o[...] = hdot_t(hdot_t(gf, w2[0]) * sig[...], w1[0])


X_SHIFT = {k: [(i, ((i // 4 + k) % 4) * 4 + i % 4) for i in range(16)] for k in (1, 2, 3)}
Y_SHIFT = {k: [(i, (i // 4) * 4 + (i + k) % 4) for i in range(8)] for k in (1, 2, 3)}
CORE = [(i, i ^ 1) for i in range(16)]
Z_LO = [(i, i ^ 2) for i in range(16)]
Z_HI = [(i, i ^ 4) for i in range(8)]


def by_x(v):
    return [lax.ppermute(v, "col", X_SHIFT[k]) for k in (1, 2, 3)]


def by_y(v):
    return [lax.ppermute(v, "row", Y_SHIFT[k]) for k in (1, 2, 3)]


def core(v):
    return lax.ppermute(v, "col", CORE)


def z_lo(v):
    return lax.ppermute(v, "col", Z_LO)


def z_hi(v):
    return lax.ppermute(v, "row", Z_HI)


def index_table(lists_c, lists_r):
    q, r = lax.axis_index("col"), lax.axis_index("row")
    mx, mzl, mco = q // 4, (q // 2) % 2, q % 2
    mz, my = r // 4, r % 4
    order = jnp.array([0, 2, 1, 3])
    own = lists_c[0]
    a, b, live = own[:, 0], own[:, 1], own[:, 2]

    def ax(t):
        return t // 4, (t // 2) % 2, t % 2

    tx, tz, tc = ax(a)
    row_idx = ((mx - tx) % 4) * 4 + (tz ^ mzl) * 2 + (tc ^ mco)
    col_idx = ((my - b % 4) % 4) * 2 + ((b // 4) ^ mz)
    agc = jnp.where(tz == mzl, (mx - tx) % 4 + 4 * (tc ^ mco), 8 + jnp.arange(2))
    agr = jnp.where(b // 4 == mz, (my - b % 4) % 4, 4 + jnp.arange(2))
    cand = lists_c.reshape(4, 4, 2, 3)[:, order]
    near = cand[0].reshape(8, 3)
    nx, nz, nc = ax(near[:, 0])
    rsc = jnp.where((near[:, 2] == 1) & (nz == mzl) & (nc == mco), (nx - mx) % 4, -1)
    nearr = lists_r[:2].reshape(4, 3)
    rsr = jnp.where(
        (nearr[:, 2] == 1) & (nearr[:, 1] // 4 == mz), (nearr[:, 1] % 4 - my) % 4, -1
    )
    px, pz, pc = ax(lists_c[2][:, 0])
    agcs = jnp.where(pz == mzl, (mx - px) % 4 + 4 * (pc ^ mco), 0)
    pb = lists_r[1][:, 1]
    agrs = jnp.where(pb // 4 == mz, (my - pb % 4) % 4, 0)
    flat_c = cand.reshape(32, 3)
    wrow = (flat_c[:, 2] == 1) & (flat_c[:, 0] == q)
    flat_r = lists_r.reshape(16, 3)
    wcol = (flat_r[:, 2] == 1) & (flat_r[:, 1] == r)
    parts = [row_idx, col_idx, live, rsc, rsr, agc, agcs, agr, agrs, wrow, wcol]
    return jnp.concatenate([p.astype(jnp.int32) for p in parts])


def body(
    positions,
    species,
    tile_list,
    pair_mask,
    embed,
    w_in,
    rbf_weight,
    rbf_bias,
    filt_weight,
    w_update1,
    w_update2,
    w_out1,
    w_out2,
):
    f32 = jnp.float32
    lists = jnp.pad(tile_list.reshape(1, 6).astype(f32), ((0, 0), (0, BLK - 6)))
    tile = jnp.concatenate(
        [positions, species.astype(f32)[None], lists, jnp.zeros((3, BLK), f32)], axis=0
    )
    far, high = lax.optimization_barrier((core(tile), z_hi(tile)))
    c2 = jnp.stack([tile, far])
    r2 = jnp.stack([tile, high])
    far, high = lax.optimization_barrier((z_lo(c2), by_y(r2)))
    c4 = jnp.concatenate([c2, far])
    c16 = jnp.concatenate([c4] + by_x(c4))
    r8 = jnp.concatenate([r2] + high)
    lists_c = c16[:, 4, :6].astype(jnp.int32).reshape(16, 2, 3)
    lists_r = r8[:, 4, :6].astype(jnp.int32).reshape(8, 2, 3)
    tab = index_table(lists_c, lists_r)
    masks = pair_mask.reshape(2, BLK, BLK)
    block = near(BLK, BLK)

    def gather_rows(v):
        four = [v] + by_x(v)
        return four, core(jnp.stack(four))

    def reduce_rows(m, name):
        m, far = lax.optimization_barrier((m, z_lo(m)))
        parts = combine_call(tab, [m, far, core(m), core(far)], T_RSC, name)
        return [parts[0]] + [lax.ppermute(parts[k], "col", X_SHIFT[k]) for k in (1, 2, 3)]

    m0, feat0, xm, fil1, q0, q1 = filter_call(
        tab, c16, r8, masks, embed, w_in, rbf_weight, rbf_bias, filt_weight
    )
    parts = reduce_rows(m0, "combine0")
    own_feat, sig0, mixed1 = call(
        up1_body,
        [block] * 3,
        None,
        [*parts, tile],
        [embed, w_update1, w_update2, w_in],
        name="update0",
    )
    four = [mixed1] + by_y(mixed1)
    sent = z_hi(select_call(tab, four, T_AGRS, "select_x"))
    m1, feat1 = call(
        msg1_body, [near(2, BLK, BLK)] * 2, tab, [*four, sent, fil1], name="msg1"
    )
    parts = reduce_rows(m1, "combine1")
    energy, gfeat2, gmsg1 = call(
        up2_body,
        [jax.ShapeDtypeStruct((1, BLK), f32), block, block],
        None,
        [*parts, own_feat],
        [w_update1, w_update2, w_out1, w_out2[None]],
        name="update1",
    )
    four, other = gather_rows(gmsg1)
    sent = z_lo(select_call(tab, [*four, other], T_AGCS, "select_g1"))
    dfeat, grad1 = call(
        dfeat_body, [near(2, BLK, BLK)] * 2, tab, [*four, other, sent, fil1], name="dfeat"
    )
    (slope1,) = call(slope1_body, [near(2, BLK, BLK)], None, [grad1, feat1, q1], name="slope1")
    far = z_hi(dfeat)
    parts = combine_call(tab, [dfeat, far], T_RSR, "combine_d")
    parts = [parts[0]] + [lax.ppermute(parts[k], "row", Y_SHIFT[k]) for k in (1, 2, 3)]
    (gmsg0,) = call(
        up3_body,
        [block],
        None,
        [*parts, gfeat2, sig0],
        [w_in, w_update1, w_update2],
        name="update2",
    )
    four, other = gather_rows(gmsg0)
    sent = z_lo(select_call(tab, [*four, other], T_AGCS, "select_g0"))
    rf, cf = call(
        force_body,
        [near(2, 8, BLK)] * 2,
        tab,
        [c16, r8, xm, slope1, *four, other, sent, q0],
        (),
        [pltpu.VMEM((2, BLK, BLK), f32)] * 2,
        name="force",
    )
    far, high = lax.optimization_barrier((z_lo(rf), z_hi(cf)))
    rf4 = jnp.concatenate([rf, far])
    cf4 = jnp.concatenate([cf, high])
    far, high = lax.optimization_barrier((core(rf4), by_y(cf4)))
    rf8 = jnp.concatenate([rf4, far])
    forces = sum_call(tab, [rf8] + by_x(rf8), [cf4] + high)
    return (energy.reshape(BLK), forces)


def solution(mesh):
    return jax.shard_map(
        body,
        mesh=mesh,
        in_specs=(
            P(None, ("row", "col")),
            P(("row", "col")),
            P("row", "col", None, None),
            P("row", "col", None, None, None),
            P(),
            P(),
            P(),
            P(),
            P(),
            P(),
            P(),
            P(),
            P(),
        ),
        out_specs=(P(("row", "col")), P(None, ("row", "col"))),
        check_vma=False,
    )
```

```python
import math

import jax
import jax.numpy as jnp
from jax import lax
from jax.experimental import pallas as pl
from jax.experimental.pallas import tpu as pltpu
from jax.sharding import PartitionSpec as P

BLK = 128
GAUSS = 256
CUTOFF = 5.0
NORM_DIV = 4.0
STEP = CUTOFF / GAUSS
LN2 = math.log(2.0)
LOG2E = 1.0 / LN2
ALPHA = math.sqrt(LOG2E / 32.0)
SLOPE = -2.0 * LN2 * ALPHA / STEP
HIGH = lax.Precision.HIGHEST
GRP = 8
SUB = 4

T_ROW, T_COL, T_LIVE = 0, 2, 4
T_RSC, T_RSR = 6, 14
T_AGC, T_AGCS, T_AGR, T_AGRS = 18, 20, 22, 24
T_WROW, T_WCOL = 26, 58


SMEM = pl.BlockSpec(memory_space=pltpu.SMEM)
VMEM = pl.BlockSpec(memory_space=pltpu.VMEM)


def near(*shape, dtype=jnp.float32):
    return pltpu.VMEM(shape, dtype)


HBM = pl.BlockSpec(memory_space=pltpu.HBM)
CHUNKS = 8
ROWS = 2 * BLK // CHUNKS
STORE = (2 * BLK, BLK, BLK)


def call(fn, outs, tab, args, weights=(), store=None, scratch=(), name=None):
    args = [pltpu.with_memory_space_constraint(a, pltpu.VMEM) for a in args]
    held = list(weights) + ([] if store is None else [store])
    held = [pltpu.with_memory_space_constraint(a, pltpu.HBM) for a in held]
    tabs = [] if tab is None else [tab]
    n_in, n_w, n_h, n_out = len(tabs) + len(args), len(weights), len(held), len(outs)

    def kernel(*refs):
        ins, far = refs[:n_in], refs[n_in : n_in + n_h]
        out = refs[n_in + n_h : n_in + n_h + n_out]
        rest = refs[n_in + n_h + n_out :]
        local, sems, extra = rest[:n_h], rest[n_h], rest[n_h + 1 :]
        copies = [pltpu.make_async_copy(far[n], local[n], sems.at[n]) for n in range(n_w)]
        for copy in copies:
            copy.start()
        feed = []
        if store is not None:

            def chunk(n):
                at = pl.ds(n * ROWS, ROWS)
                return pltpu.make_async_copy(far[-1].at[at], local[-1].at[at], sems.at[n_w + n])

            for n in range(CHUNKS):
                chunk(n).start()
            feed = [chunk]
        for copy in copies:
            copy.wait()
        fn(*ins, *local, *out, *extra, *feed)

    return pl.pallas_call(
        kernel,
        out_shape=list(outs),
        in_specs=[SMEM] * len(tabs) + [VMEM] * len(args) + [HBM] * n_h,
        out_specs=[HBM if getattr(o, "memory_space", None) == pltpu.HBM else VMEM for o in outs],
        scratch_shapes=[pltpu.VMEM(a.shape, a.dtype) for a in held]
        + [pltpu.SemaphoreType.DMA((max(n_w + (CHUNKS if store is not None else 0), 1),))]
        + list(scratch),
        compiler_params=pltpu.CompilerParams(vmem_limit_bytes=24 << 20),
        name=name,
    )(*tabs, *args, *held)


def hdot(a, b):
    return jnp.dot(a, b, precision=HIGH, preferred_element_type=jnp.float32)


def hdot_t(a, b):
    return lax.dot_general(
        a, b, (((1,), (1,)), ((), ())), precision=HIGH, preferred_element_type=jnp.float32
    )


def ssp_sig(v):
    e = jnp.exp(-jnp.abs(v))
    act = jnp.maximum(v, 0.0) + jnp.log(1.0 + e) - LN2
    sig = jnp.where(v >= 0.0, 1.0, e) / (1.0 + e)
    return act, sig


def feature_rows(tile, embed):
    spec = jnp.transpose(tile)[:, 3:4]
    kinds = lax.broadcasted_iota(jnp.int32, (BLK, embed.shape[0]), 1).astype(jnp.float32)
    onehot = jnp.where(spec == kinds, 1.0, 0.0)
    return hdot(onehot, embed)


def turn(mat, base):
    return pltpu.roll(mat, lax.rem(BLK - base, BLK), axis=1)


def spread(turned, ks, width):
    return jnp.concatenate(
        [jnp.broadcast_to(turned[:, k : k + 1], (BLK, width)) for k in ks], axis=0
    )


def filter_body(
    tab, c16, r8, mask, embed, w_in, w_rbf, b_rbf, w_fil, m_o, feat_o, x_o, fil_o, q0_o, q1_o,
    cm_s, dcm_s, w_s, buf_s, out_sem,
):
    for s in range(2):
        rt = c16[tab[T_ROW + s]]
        ct = r8[tab[T_COL + s]]
        ctt = jnp.transpose(ct)
        d2 = jnp.zeros((BLK, BLK), jnp.float32)
        for a in range(3):
            off = rt[a : a + 1, :] - ctt[:, a : a + 1]
            d2 = d2 + off * off
        d = jnp.sqrt(d2 + 0.01)
        live = (tab[T_LIVE + s]).astype(jnp.float32) * (LN2 / NORM_DIV)
        gate = jnp.transpose(mask[s].astype(jnp.float32)) * live
        ang = d * (math.pi / CUTOFF)
        near_by = d < CUTOFF
        x_o[s] = d * (ALPHA / STEP)
        cm_s[s] = jnp.where(near_by, 0.5 * (jnp.cos(ang) + 1.0), 0.0) * gate
        dcm_s[s] = jnp.where(near_by, (-0.5 * math.pi / CUTOFF) * jnp.sin(ang), 0.0) * gate
        feat_o[s] = hdot(feature_rows(ct, embed[...]), w_in[0])
    w_s[:, :BLK] = w_rbf[0]
    w_s[:, BLK:] = w_rbf[1]
    stores = (fil_o, q0_o, q1_o)

    def save(it, n):
        slot = lax.rem(it, 2)
        return pltpu.make_async_copy(
            buf_s.at[slot, n], stores[n].at[pl.ds(it * GRP, GRP)], out_sem.at[slot, n]
        )

    def step(it, _):
        s, base = place(it)
        slot = lax.rem(it, 2)

        @pl.when(it >= 2)
        def _():
            for n in range(3):
                save(it - 2, n).wait()

        xt, ct, dt = turn(x_o[s], base), turn(cm_s[s], base), turn(dcm_s[s], base)
        feats = feat_o[s]
        ticks = lax.broadcasted_iota(jnp.int32, (1, GAUSS), 1).astype(jnp.float32) * ALPHA
        bias = jnp.concatenate([b_rbf[0:1], b_rbf[1:2]], axis=1) * LOG2E
        rows = []
        for first in range(0, GRP, SUB):
            ks = range(first, first + SUB)
            u = spread(xt, ks, GAUSS) - ticks
            ex = jnp.exp2(math.log2(LOG2E) - u * u)
            pre = jnp.dot(ex.astype(jnp.bfloat16), w_s[...], preferred_element_type=jnp.float32)
            dpre = jnp.dot(
                (u * ex).astype(jnp.bfloat16), w_s[...], preferred_element_type=jnp.float32
            )
            c = spread(ct, ks, BLK)
            cd = c * (SLOPE / (LN2 * LOG2E))
            dc = spread(dt, ks, BLK)
            for layer in range(2):
                cols = slice(layer * BLK, (layer + 1) * BLK)
                p2 = pre[:, cols] + bias[:, cols]
                lg = jnp.log2(1.0 + jnp.exp2(p2))
                hid = lg - 1.0
                mix = dc * hid + cd * (jnp.exp2(p2 - lg) * dpre[:, cols])
                both = jnp.concatenate([hid.astype(jnp.bfloat16), mix.astype(jnp.bfloat16)], axis=0)
                both = jnp.dot(both, w_fil[layer], preferred_element_type=jnp.float32)
                fil = both[: SUB * BLK] * c
                slope = both[SUB * BLK :].reshape(SUB, BLK, BLK)
                at = pl.ds(first, SUB)
                if layer == 0:
                    for k in range(SUB):
                        here = slice(k * BLK, (k + 1) * BLK)
                        rows.append(jnp.sum(fil[here] * feats, axis=0, keepdims=True))
                    buf_s[slot, 1, at] = (slope * feats[None]).astype(jnp.bfloat16)
                else:
                    buf_s[slot, 0, at] = fil.astype(jnp.bfloat16).reshape(SUB, BLK, BLK)
                    buf_s[slot, 2, at] = slope.astype(jnp.bfloat16)
        m_o[s, pl.ds(base, GRP), :] = jnp.concatenate(rows, axis=0)
        for n in range(3):
            save(it, n).start()
        return 0

    steps = 2 * BLK // GRP
    lax.fori_loop(0, steps, step, 0)
    for it in (steps - 2, steps - 1):
        for n in range(3):
            save(it, n).wait()


def filter_call(tab, c16, r8, mask, embed, w_in, w_rbf, b_rbf, w_fil):
    big = pltpu.HBM(STORE, jnp.bfloat16)
    return call(
        filter_body,
        [near(2, BLK, BLK)] * 3 + [big] * 3,
        tab,
        [c16, r8],
        [mask, embed, w_in, w_rbf, b_rbf, w_fil],
        scratch=[pltpu.VMEM((2, BLK, BLK), jnp.float32)] * 2
        + [
            pltpu.VMEM((GAUSS, 2 * BLK), jnp.bfloat16),
            pltpu.VMEM((2, 3, GRP, BLK, BLK), jnp.bfloat16),
            pltpu.SemaphoreType.DMA((2, 3)),
        ],
        name="filters",
    )


def pick(code, sources, store):
    for n, read in enumerate(sources):

        @pl.when(code == n)
        def _(read=read):
            store(read())


def readers(refs):
    out = []
    for ref in refs:
        if len(ref.shape) == 2:
            out.append(lambda ref=ref: ref[...])
        else:
            out.extend([lambda ref=ref, n=n: ref[n] for n in range(ref.shape[0])])
    return out


def select_body(tab, *refs, at):
    sources, o = readers(refs[:-1]), refs[-1]
    for s in range(2):

        def store(v, s=s):
            o[s] = v

        pick(tab[at + s], sources, store)


def select_call(tab, blocks, at, name):
    return call(
        lambda *refs: select_body(*refs, at=at), [near(2, BLK, BLK)], tab, blocks, name=name
    )[0]


def combine_body(tab, *refs, at):
    sources, outs = readers(refs[:-4]), refs[-4:]
    for o in outs:
        o[...] = jnp.zeros_like(o)
    for n, read in enumerate(sources):
        for k, o in enumerate(outs):

            @pl.when(tab[at + n] == k)
            def _(read=read, o=o):
                o[...] += read()


def combine_call(tab, blocks, at, name):
    return call(
        lambda *refs: combine_body(*refs, at=at), [near(BLK, BLK)] * 4, tab, blocks, name=name
    )


def resolve(tab, at, refs, scratch):
    sources = readers(refs)
    for s in range(2):

        def store(v, s=s):
            scratch[s] = v

        pick(tab[at + s], sources, store)


def place(it):
    return it // (BLK // GRP), pl.multiple_of(lax.rem(it, BLK // GRP) * GRP, GRP)


def loop(fn, chunk, first=0, last=CHUNKS):
    per = ROWS // GRP

    def step(it, carry):
        @pl.when(lax.rem(it, per) == 0)
        def _():
            chunk(it // per).wait()

        fn(it)
        return carry

    lax.fori_loop(first * per, last * per, step, 0)


def msg1_body(tab, *refs):
    src, fil, o, feat_o, chunk = refs[:-4], *refs[-4:]
    resolve(tab, T_AGR, src, feat_o)

    def step(it):
        s, base = place(it)
        feats = feat_o[s]
        rows = [
            jnp.sum(fil[it * GRP + k].astype(jnp.float32) * feats, axis=0, keepdims=True)
            for k in range(GRP)
        ]
        o[s, pl.ds(base, GRP), :] = jnp.concatenate(rows, axis=0)

    loop(step, chunk)


def dfeat_body(tab, *refs):
    src, fil, o, grad_o, chunk = refs[:-4], *refs[-4:]
    resolve(tab, T_AGC, src, grad_o)
    o[...] = jnp.zeros_like(o)

    def step(it):
        s, base = place(it)
        rows = grad_o[s, pl.ds(base, GRP), :]
        acc = o[s]
        for k in range(GRP):
            acc = acc + fil[it * GRP + k].astype(jnp.float32) * rows[k : k + 1, :]
        o[s] = acc

    loop(step, chunk)


def slope_step(it, store, grads, feats, o):
    s, base = place(it)
    lanes = lax.broadcasted_iota(jnp.int32, (BLK, BLK), 1)
    rows = store[pl.ds(it * GRP, GRP)]
    if feats is not None:
        rows = rows * feats[s].astype(jnp.bfloat16)[None]
    prod = lax.dot_general(
        rows.reshape(GRP * BLK, BLK),
        grads[s].astype(jnp.bfloat16),
        (((1,), (1,)), ((), ())),
        preferred_element_type=jnp.float32,
    )
    acc = o[s]
    for k in range(GRP):
        acc = jnp.where(lanes == base + k, prod[k * BLK : (k + 1) * BLK], acc)
    o[s] = acc


def slope1_body(grads, feats, store, o, chunk):
    o[...] = jnp.zeros_like(o)
    loop(lambda it: slope_step(it, store, grads, feats, o), chunk)


def force_body(tab, c16, r8, xm, first, *refs):
    src, store, rf_o, cf_o, grad_s, acc_s, chunk = refs[:-6], *refs[-6:]
    resolve(tab, T_AGC, src, grad_s)
    acc_s[...] = jnp.zeros_like(acc_s)
    loop(lambda it: slope_step(it, store, grad_s, None, acc_s), chunk)
    for s in range(2):
        rt = c16[tab[T_ROW + s]]
        ctt = jnp.transpose(r8[tab[T_COL + s]])
        pull = -(first[s] + acc_s[s]) / (xm[s] * (STEP / ALPHA))
        rows, cols = [], []
        for a in range(3):
            comp = pull * (rt[a : a + 1, :] - ctt[:, a : a + 1])
            rows.append(jnp.sum(comp, axis=0, keepdims=True))
            cols.append(jnp.sum(comp, axis=1, keepdims=True))
        rf_o[s] = jnp.concatenate(rows + [jnp.zeros((5, BLK), jnp.float32)], axis=0)
        cols = jnp.concatenate(cols + [jnp.zeros((BLK, BLK - 3), jnp.float32)], axis=1)
        cf_o[s] = -jnp.transpose(cols)[:8]


def sum_body(tab, *refs):
    rows, cols, o = refs[:4], refs[4:8], refs[8]
    acc = jnp.zeros((8, BLK), jnp.float32)
    for n in range(32):
        acc = acc + rows[n // 8][n % 8] * tab[T_WROW + n].astype(jnp.float32)
    for n in range(16):
        acc = acc + cols[n // 4][n % 4] * tab[T_WCOL + n].astype(jnp.float32)
    o[...] = acc[:3]


def sum_call(tab, rows, cols):
    args = [pltpu.with_memory_space_constraint(a, pltpu.VMEM) for a in (*rows, *cols)]
    return pl.pallas_call(
        sum_body,
        out_shape=jax.ShapeDtypeStruct((3, BLK), jnp.float32),
        in_specs=[SMEM] + [VMEM] * 8,
        out_specs=VMEM,
        name="sum_forces",
    )(tab, *args)


def up1_body(m0, m1, m2, m3, tile, embed, w1, w2, w_in, feat_o, sig_o, mixed_o):
    message = (m0[...] + m1[...]) + (m2[...] + m3[...])
    act, sig = ssp_sig(hdot(message, w1[0]))
    feats = feature_rows(tile[...], embed[...]) + hdot(act, w2[0])
    feat_o[...] = feats
    sig_o[...] = sig
    mixed_o[...] = hdot(feats, w_in[1])


def up2_body(m0, m1, m2, m3, feat, w1, w2, wo1, wo2, en_o, gfeat_o, gmsg_o):
    message = (m0[...] + m1[...]) + (m2[...] + m3[...])
    act, sig = ssp_sig(hdot(message, w1[1]))
    feats = feat[...] + hdot(act, w2[1])
    head, head_sig = ssp_sig(hdot(feats, wo1[...]))
    en_o[...] = hdot_t(jnp.broadcast_to(wo2[...], (8, wo2.shape[1])), head)[:1]
    gfeat = hdot_t(head_sig * wo2[...], wo1[...])
    gfeat_o[...] = gfeat
    gmsg_o[...] = hdot_t(hdot_t(gfeat, w2[1]) * sig, w1[1])


def up3_body(m0, m1, m2, m3, gfeat, sig, w_in, w1, w2, gmsg_o):
    total = (m0[...] + m1[...]) + (m2[...] + m3[...])
    gf = gfeat[...] + hdot_t(total, w_in[1])
    gmsg_o[...] = hdot_t(hdot_t(gf, w2[0]) * sig[...], w1[0])


X_SHIFT = {k: [(i, ((i // 4 + k) % 4) * 4 + i % 4) for i in range(16)] for k in (1, 2, 3)}
Y_SHIFT = {k: [(i, (i // 4) * 4 + (i + k) % 4) for i in range(8)] for k in (1, 2, 3)}
CORE = [(i, i ^ 1) for i in range(16)]
Z_LO = [(i, i ^ 2) for i in range(16)]
Z_HI = [(i, i ^ 4) for i in range(8)]


def by_x(v):
    return [lax.ppermute(v, "col", X_SHIFT[k]) for k in (1, 2, 3)]


def by_y(v):
    return [lax.ppermute(v, "row", Y_SHIFT[k]) for k in (1, 2, 3)]


def core(v):
    return lax.ppermute(v, "col", CORE)


def z_lo(v):
    return lax.ppermute(v, "col", Z_LO)


def z_hi(v):
    return lax.ppermute(v, "row", Z_HI)


def index_table(lists_c, lists_r):
    q, r = lax.axis_index("col"), lax.axis_index("row")
    mx, mzl, mco = q // 4, (q // 2) % 2, q % 2
    mz, my = r // 4, r % 4
    order = jnp.array([0, 2, 1, 3])
    own = lists_c[0]
    a, b, live = own[:, 0], own[:, 1], own[:, 2]

    def ax(t):
        return t // 4, (t // 2) % 2, t % 2

    tx, tz, tc = ax(a)
    row_idx = ((mx - tx) % 4) * 4 + (tz ^ mzl) * 2 + (tc ^ mco)
    col_idx = ((my - b % 4) % 4) * 2 + ((b // 4) ^ mz)
    agc = jnp.where(tz == mzl, (mx - tx) % 4 + 4 * (tc ^ mco), 8 + jnp.arange(2))
    agr = jnp.where(b // 4 == mz, (my - b % 4) % 4, 4 + jnp.arange(2))
    cand = lists_c.reshape(4, 4, 2, 3)[:, order]
    near = cand[0].reshape(8, 3)
    nx, nz, nc = ax(near[:, 0])
    rsc = jnp.where((near[:, 2] == 1) & (nz == mzl) & (nc == mco), (nx - mx) % 4, -1)
    nearr = lists_r[:2].reshape(4, 3)
    rsr = jnp.where(
        (nearr[:, 2] == 1) & (nearr[:, 1] // 4 == mz), (nearr[:, 1] % 4 - my) % 4, -1
    )
    px, pz, pc = ax(lists_c[2][:, 0])
    agcs = jnp.where(pz == mzl, (mx - px) % 4 + 4 * (pc ^ mco), 0)
    pb = lists_r[1][:, 1]
    agrs = jnp.where(pb // 4 == mz, (my - pb % 4) % 4, 0)
    flat_c = cand.reshape(32, 3)
    wrow = (flat_c[:, 2] == 1) & (flat_c[:, 0] == q)
    flat_r = lists_r.reshape(16, 3)
    wcol = (flat_r[:, 2] == 1) & (flat_r[:, 1] == r)
    parts = [row_idx, col_idx, live, rsc, rsr, agc, agcs, agr, agrs, wrow, wcol]
    return jnp.concatenate([p.astype(jnp.int32) for p in parts])


def body(
    positions,
    species,
    tile_list,
    pair_mask,
    embed,
    w_in,
    rbf_weight,
    rbf_bias,
    filt_weight,
    w_update1,
    w_update2,
    w_out1,
    w_out2,
):
    f32 = jnp.float32
    lists = jnp.pad(tile_list.reshape(1, 6).astype(f32), ((0, 0), (0, BLK - 6)))
    tile = jnp.concatenate(
        [positions, species.astype(f32)[None], lists, jnp.zeros((3, BLK), f32)], axis=0
    )
    far, high = lax.optimization_barrier((core(tile), z_hi(tile)))
    c2 = jnp.stack([tile, far])
    r2 = jnp.stack([tile, high])
    far, high = lax.optimization_barrier((z_lo(c2), by_y(r2)))
    c4 = jnp.concatenate([c2, far])
    c16 = jnp.concatenate([c4] + by_x(c4))
    r8 = jnp.concatenate([r2] + high)
    lists_c = c16[:, 4, :6].astype(jnp.int32).reshape(16, 2, 3)
    lists_r = r8[:, 4, :6].astype(jnp.int32).reshape(8, 2, 3)
    tab = index_table(lists_c, lists_r)
    masks = pair_mask.reshape(2, BLK, BLK)
    block = near(BLK, BLK)

    def gather_rows(v):
        four = [v] + by_x(v)
        return four, core(jnp.stack(four))

    def reduce_rows(m, name):
        m, far = lax.optimization_barrier((m, z_lo(m)))
        parts = combine_call(tab, [m, far, core(m), core(far)], T_RSC, name)
        return [parts[0]] + [lax.ppermute(parts[k], "col", X_SHIFT[k]) for k in (1, 2, 3)]

    m0, feat0, xm, fil1, q0, q1 = filter_call(
        tab, c16, r8, masks, embed, w_in, rbf_weight, rbf_bias, filt_weight
    )
    parts = reduce_rows(m0, "combine0")
    own_feat, sig0, mixed1 = call(
        up1_body,
        [block] * 3,
        None,
        [*parts, tile],
        [embed, w_update1, w_update2, w_in],
        name="update0",
    )
    four = [mixed1] + by_y(mixed1)
    sent = z_hi(select_call(tab, four, T_AGRS, "select_x"))
    m1, feat1 = call(
        msg1_body, [near(2, BLK, BLK)] * 2, tab, [*four, sent], store=fil1, name="msg1"
    )
    parts = reduce_rows(m1, "combine1")
    energy, gfeat2, gmsg1 = call(
        up2_body,
        [jax.ShapeDtypeStruct((1, BLK), f32), block, block],
        None,
        [*parts, own_feat],
        [w_update1, w_update2, w_out1, w_out2[None]],
        name="update1",
    )
    four, other = gather_rows(gmsg1)
    sent = z_lo(select_call(tab, [*four, other], T_AGCS, "select_g1"))
    dfeat, grad1 = call(
        dfeat_body, [near(2, BLK, BLK)] * 2, tab, [*four, other, sent], store=fil1, name="dfeat"
    )
    (slope1,) = call(
        slope1_body, [near(2, BLK, BLK)], None, [grad1, feat1], store=q1, name="slope1"
    )
    far, slope1 = lax.optimization_barrier((z_hi(dfeat), slope1))
    parts = combine_call(tab, [dfeat, far], T_RSR, "combine_d")
    parts = [parts[0]] + [lax.ppermute(parts[k], "row", Y_SHIFT[k]) for k in (1, 2, 3)]
    (gmsg0,) = call(
        up3_body,
        [block],
        None,
        [*parts, gfeat2, sig0],
        [w_in, w_update1, w_update2],
        name="update2",
    )
    four, other = gather_rows(gmsg0)
    sent = z_lo(select_call(tab, [*four, other], T_AGCS, "select_g0"))
    rf, cf = call(
        force_body,
        [near(2, 8, BLK)] * 2,
        tab,
        [c16, r8, xm, slope1, *four, other, sent],
        store=q0,
        scratch=[pltpu.VMEM((2, BLK, BLK), f32)] * 2,
        name="force",
    )
    far, high = lax.optimization_barrier((z_lo(rf), z_hi(cf)))
    rf4 = jnp.concatenate([rf, far])
    cf4 = jnp.concatenate([cf, high])
    far, high = lax.optimization_barrier((core(rf4), by_y(cf4)))
    rf8 = jnp.concatenate([rf4, far])
    forces = sum_call(tab, [rf8] + by_x(rf8), [cf4] + high)
    return (energy.reshape(BLK), forces)


def solution(mesh):
    return jax.shard_map(
        body,
        mesh=mesh,
        in_specs=(
            P(None, ("row", "col")),
            P(("row", "col")),
            P("row", "col", None, None),
            P("row", "col", None, None, None),
            P(),
            P(),
            P(),
            P(),
            P(),
            P(),
            P(),
            P(),
            P(),
        ),
        out_specs=(P(("row", "col")), P(None, ("row", "col"))),
        check_vma=False,
    )
```

```python
import math

import jax
import jax.numpy as jnp
from jax import lax
from jax.experimental import pallas as pl
from jax.experimental.pallas import tpu as pltpu
from jax.sharding import PartitionSpec as P

BLK = 128
GAUSS = 256
CUTOFF = 5.0
NORM_DIV = 4.0
STEP = CUTOFF / GAUSS
LN2 = math.log(2.0)
LOG2E = 1.0 / LN2
ALPHA = math.sqrt(LOG2E / 32.0)
SLOPE = -2.0 * LN2 * ALPHA / STEP
HIGH = lax.Precision.HIGHEST
GRP = 8
SUB = 4

T_ROW, T_COL, T_LIVE = 0, 2, 4
T_RSC, T_RSR = 6, 14
T_AGC, T_AGCS, T_AGR, T_AGRS = 18, 20, 22, 24
T_WROW, T_WCOL = 0, 32


SMEM = pl.BlockSpec(memory_space=pltpu.SMEM)
VMEM = pl.BlockSpec(memory_space=pltpu.VMEM)


def near(*shape, dtype=jnp.float32):
    return pltpu.VMEM(shape, dtype)


HBM = pl.BlockSpec(memory_space=pltpu.HBM)
CHUNKS = 8
ROWS = 2 * BLK // CHUNKS
STORE = (2 * BLK, BLK, BLK)


def call(fn, outs, tab, args, weights=(), store=None, rows=(0, BLK), scratch=(), name=None):
    args = [pltpu.with_memory_space_constraint(a, pltpu.VMEM) for a in args]
    held = list(weights) + ([] if store is None else [store])
    held = [pltpu.with_memory_space_constraint(a, pltpu.HBM) for a in held]
    tabs = [] if tab is None else [tab]
    n_in, n_w, n_h, n_out = len(tabs) + len(args), len(weights), len(held), len(outs)

    def kernel(*refs):
        ins, far = refs[:n_in], refs[n_in : n_in + n_h]
        out = refs[n_in + n_h : n_in + n_h + n_out]
        rest = refs[n_in + n_h + n_out :]
        local, sems, extra = rest[:n_h], rest[n_h], rest[n_h + 1 :]
        copies = [pltpu.make_async_copy(far[n], local[n], sems.at[n]) for n in range(n_w)]
        for copy in copies:
            copy.start()
        feed = []
        if store is not None:

            def chunk(n):
                at = pl.ds(n * ROWS, ROWS)
                return pltpu.make_async_copy(far[-1].at[at], local[-1].at[at], sems.at[n_w + n])

            for n in range((rows[1] - rows[0]) // ROWS):
                for row in rows:
                    chunk(row // ROWS + n).start()
            feed = [lambda step: stream(step, chunk, rows)]
        for copy in copies:
            copy.wait()
        fn(*ins, *local, *out, *extra, *feed)

    return pl.pallas_call(
        kernel,
        out_shape=list(outs),
        in_specs=[SMEM] * len(tabs) + [VMEM] * len(args) + [HBM] * n_h,
        out_specs=[HBM if getattr(o, "memory_space", None) == pltpu.HBM else VMEM for o in outs],
        scratch_shapes=[pltpu.VMEM(a.shape, a.dtype) for a in held]
        + [pltpu.SemaphoreType.DMA((max(n_w + (CHUNKS if store is not None else 0), 1),))]
        + list(scratch),
        compiler_params=pltpu.CompilerParams(vmem_limit_bytes=24 << 20),
        name=name,
    )(*tabs, *args, *held)


def stream(fn, chunk, rows):
    per = ROWS // GRP

    def step(it, carry):
        @pl.when(lax.rem(it, per) == 0)
        def _():
            for row in rows:
                chunk(row // ROWS + it // per).wait()

        for half, row in enumerate(rows):
            fn(row // BLK, pl.multiple_of(row % BLK + it * GRP, GRP), half)
        return carry

    lax.fori_loop(0, (rows[1] - rows[0]) // GRP, step, 0)


def hdot(a, b):
    return jnp.dot(a, b, precision=HIGH, preferred_element_type=jnp.float32)


def hdot_t(a, b):
    return lax.dot_general(
        a, b, (((1,), (1,)), ((), ())), precision=HIGH, preferred_element_type=jnp.float32
    )


def ssp_sig(v):
    e = jnp.exp(-jnp.abs(v))
    act = jnp.maximum(v, 0.0) + jnp.log(1.0 + e) - LN2
    sig = jnp.where(v >= 0.0, 1.0, e) / (1.0 + e)
    return act, sig


def feature_rows(tile, embed):
    spec = jnp.transpose(tile)[:, 3:4]
    kinds = lax.broadcasted_iota(jnp.int32, (BLK, embed.shape[0]), 1).astype(jnp.float32)
    onehot = jnp.where(spec == kinds, 1.0, 0.0)
    return hdot(onehot, embed)


def turn(mat, base):
    return pltpu.roll(mat, lax.rem(BLK - base, BLK), axis=1)


def spread(turned, ks, width):
    return jnp.concatenate(
        [jnp.broadcast_to(turned[:, k : k + 1], (BLK, width)) for k in ks], axis=0
    )


def filter_body(
    tab, c16, r8, mask, embed, w_in, w_rbf, b_rbf, w_fil, m_o, feat_o, x_o, fil_o, q0_o, q1_o,
    cm_s, dcm_s, w_s, buf_s, out_sem,
):
    for s in range(2):
        rt = c16[tab[T_ROW + s]]
        ct = r8[tab[T_COL + s]]
        ctt = jnp.transpose(ct)
        d2 = jnp.zeros((BLK, BLK), jnp.float32)
        for a in range(3):
            off = rt[a : a + 1, :] - ctt[:, a : a + 1]
            d2 = d2 + off * off
        d = jnp.sqrt(d2 + 0.01)
        live = (tab[T_LIVE + s]).astype(jnp.float32) * (LN2 / NORM_DIV)
        gate = jnp.transpose(mask[s].astype(jnp.float32)) * live
        ang = d * (math.pi / CUTOFF)
        near_by = d < CUTOFF
        x_o[s] = d * (ALPHA / STEP)
        cm_s[s] = jnp.where(near_by, 0.5 * (jnp.cos(ang) + 1.0), 0.0) * gate
        dcm_s[s] = jnp.where(near_by, (-0.5 * math.pi / CUTOFF) * jnp.sin(ang), 0.0) * gate
        feat_o[s] = hdot(feature_rows(ct, embed[...]), w_in[0])
    w_s[:, :BLK] = w_rbf[0]
    w_s[:, BLK:] = w_rbf[1]
    stores = (fil_o, q0_o, q1_o)

    def save(it, n):
        slot = lax.rem(it, 2)
        return pltpu.make_async_copy(
            buf_s.at[slot, n], stores[n].at[pl.ds(it * GRP, GRP)], out_sem.at[slot, n]
        )

    def step(it, _):
        s, base = place(it)
        slot = lax.rem(it, 2)

        @pl.when(it >= 2)
        def _():
            for n in range(3):
                save(it - 2, n).wait()

        xt, ct, dt = turn(x_o[s], base), turn(cm_s[s], base), turn(dcm_s[s], base)
        feats = feat_o[s]
        ticks = lax.broadcasted_iota(jnp.int32, (1, GAUSS), 1).astype(jnp.float32) * ALPHA
        bias = jnp.concatenate([b_rbf[0:1], b_rbf[1:2]], axis=1) * LOG2E - 1.0
        rows = []
        for first in range(0, GRP, SUB):
            ks = range(first, first + SUB)
            u = spread(xt, ks, GAUSS) - ticks
            ex = jnp.exp2(math.log2(LOG2E) - u * u)
            pre = jnp.dot(ex.astype(jnp.bfloat16), w_s[...], preferred_element_type=jnp.float32)
            dpre = jnp.dot(
                (u * ex).astype(jnp.bfloat16), w_s[...], preferred_element_type=jnp.float32
            )
            c = spread(ct, ks, BLK)
            cd = c * (SLOPE / (LN2 * LOG2E))
            dc = spread(dt, ks, BLK)
            for layer in range(2):
                cols = slice(layer * BLK, (layer + 1) * BLK)
                p2 = pre[:, cols] + bias[:, cols]
                hid = jnp.log2(0.5 + jnp.exp2(p2))
                mix = dc * hid + cd * (jnp.exp2(p2 - hid) * dpre[:, cols])
                both = jnp.concatenate([hid.astype(jnp.bfloat16), mix.astype(jnp.bfloat16)], axis=0)
                both = jnp.dot(both, w_fil[layer], preferred_element_type=jnp.float32)
                fil = both[: SUB * BLK] * c
                slope = both[SUB * BLK :].reshape(SUB, BLK, BLK)
                at = pl.ds(first, SUB)
                if layer == 0:
                    for k in range(SUB):
                        here = slice(k * BLK, (k + 1) * BLK)
                        rows.append(jnp.sum(fil[here] * feats, axis=0, keepdims=True))
                    buf_s[slot, 1, at] = (slope * feats[None]).astype(jnp.bfloat16)
                else:
                    buf_s[slot, 0, at] = fil.astype(jnp.bfloat16).reshape(SUB, BLK, BLK)
                    buf_s[slot, 2, at] = slope.astype(jnp.bfloat16)
        m_o[s, pl.ds(base, GRP), :] = jnp.concatenate(rows, axis=0)
        for n in range(3):
            save(it, n).start()
        return 0

    steps = 2 * BLK // GRP
    lax.fori_loop(0, steps, step, 0)
    for it in (steps - 2, steps - 1):
        for n in range(3):
            save(it, n).wait()


def filter_call(tab, c16, r8, mask, embed, w_in, w_rbf, b_rbf, w_fil):
    big = pltpu.HBM(STORE, jnp.bfloat16)
    return call(
        filter_body,
        [near(2, BLK, BLK)] * 3 + [big] * 3,
        tab,
        [c16, r8],
        [mask, embed, w_in, w_rbf, b_rbf, w_fil],
        scratch=[pltpu.VMEM((2, BLK, BLK), jnp.float32)] * 2
        + [
            pltpu.VMEM((GAUSS, 2 * BLK), jnp.bfloat16),
            pltpu.VMEM((2, 3, GRP, BLK, BLK), jnp.bfloat16),
            pltpu.SemaphoreType.DMA((2, 3)),
        ],
        name="filters",
    )


def pick(code, sources, store):
    for n, read in enumerate(sources):

        @pl.when(code == n)
        def _(read=read):
            store(read())


def readers(refs):
    out = []
    for ref in refs:
        if len(ref.shape) == 2:
            out.append(lambda ref=ref: ref[...])
        else:
            out.extend([lambda ref=ref, n=n: ref[n] for n in range(ref.shape[0])])
    return out


def select_body(tab, *refs, at):
    sources, o = readers(refs[:-1]), refs[-1]
    for s in range(2):

        def store(v, s=s):
            o[s] = v

        pick(tab[at + s], sources, store)


def select_call(tab, blocks, at, name):
    return call(
        lambda *refs: select_body(*refs, at=at), [near(2, BLK, BLK)], tab, blocks, name=name
    )[0]


def combine_body(tab, *refs, at):
    sources, outs = readers(refs[:-4]), refs[-4:]
    for o in outs:
        o[...] = jnp.zeros_like(o)
    for n, read in enumerate(sources):
        for k, o in enumerate(outs):

            @pl.when(tab[at + n] == k)
            def _(read=read, o=o):
                o[...] += read()


def combine_call(tab, blocks, at, name):
    return call(
        lambda *refs: combine_body(*refs, at=at), [near(BLK, BLK)] * 4, tab, blocks, name=name
    )


def resolve(tab, at, refs, scratch):
    sources = readers(refs)
    for s in range(2):

        def store(v, s=s):
            scratch[s] = v

        pick(tab[at + s], sources, store)


def place(it):
    return it // (BLK // GRP), pl.multiple_of(lax.rem(it, BLK // GRP) * GRP, GRP)


def msg1_body(tab, *refs):
    src, fil, o, feat_o, loop = refs[:-4], *refs[-4:]
    resolve(tab, T_AGR, src, feat_o)

    def step(s, base, half):
        feats = feat_o[s]
        rows = [
            jnp.sum(fil[s * BLK + base + k].astype(jnp.float32) * feats, axis=0, keepdims=True)
            for k in range(GRP)
        ]
        o[s, pl.ds(base, GRP), :] = jnp.concatenate(rows, axis=0)

    loop(step)


def dfeat_body(tab, *refs):
    src, fil, o, grad_o, loop = refs[:-4], *refs[-4:]
    resolve(tab, T_AGC, src, grad_o)
    o[...] = jnp.zeros_like(o)

    def step(s, base, half):
        rows = grad_o[s, pl.ds(base, GRP), :]
        acc = o[s]
        for k in range(GRP):
            acc = acc + fil[s * BLK + base + k].astype(jnp.float32) * rows[k : k + 1, :]
        o[s] = acc

    loop(step)


def slope_step(s, base, store, turned, feats, o, out):
    lanes = lax.broadcasted_iota(jnp.int32, (BLK, BLK), 1)
    rows = store[pl.ds(s * BLK + base, GRP)]
    if feats is not None:
        rows = rows * feats[s].astype(jnp.bfloat16)[None]
    prod = jnp.dot(
        rows.reshape(GRP * BLK, BLK), turned[s], preferred_element_type=jnp.float32
    )
    acc = o[out]
    for k in range(GRP):
        acc = jnp.where(lanes == base + k, prod[k * BLK : (k + 1) * BLK], acc)
    o[out] = acc


def slope1_body(grads, feats, store, o, turned, acc, loop, *, slot):
    turned[slot] = jnp.transpose(grads[slot]).astype(jnp.bfloat16)
    acc[...] = jnp.zeros_like(acc)
    loop(
        lambda s, base, half: slope_step(s, base, store, turned, feats, acc, half)
    )
    o[...] = acc[0] + acc[1]


def force_body(tab, c16, r8, xm, first0, first1, *refs):
    src, store, rf_o, cf_o, grad_s, acc_s, turned, loop = refs[:-7], *refs[-7:]
    resolve(tab, T_AGC, src, grad_s)
    acc_s[...] = jnp.zeros_like(acc_s)
    for s in range(2):
        turned[s] = jnp.transpose(grad_s[s]).astype(jnp.bfloat16)
    loop(lambda s, base, half: slope_step(s, base, store, turned, None, acc_s, half))
    for s, first in enumerate((first0, first1)):
        rt = c16[tab[T_ROW + s]]
        ctt = jnp.transpose(r8[tab[T_COL + s]])
        pull = -(first[...] + acc_s[s]) / (xm[s] * (STEP / ALPHA))
        rows, cols = [], []
        for a in range(3):
            comp = pull * (rt[a : a + 1, :] - ctt[:, a : a + 1])
            rows.append(jnp.sum(comp, axis=0, keepdims=True))
            cols.append(jnp.sum(comp, axis=1, keepdims=True))
        rf_o[s] = jnp.concatenate(rows + [jnp.zeros((5, BLK), jnp.float32)], axis=0)
        cols = jnp.concatenate(cols + [jnp.zeros((BLK, BLK - 3), jnp.float32)], axis=1)
        cf_o[s] = -jnp.transpose(cols)[:8]


def sum_body(tab, *refs):
    rows, cols, o = refs[:4], refs[4:8], refs[8]
    acc = jnp.zeros((8, BLK), jnp.float32)
    for n in range(32):
        acc = acc + rows[n // 8][n % 8] * tab[T_WROW + n].astype(jnp.float32)
    for n in range(16):
        acc = acc + cols[n // 4][n % 4] * tab[T_WCOL + n].astype(jnp.float32)
    o[...] = acc[:3]


def sum_call(tab, rows, cols):
    args = [pltpu.with_memory_space_constraint(a, pltpu.VMEM) for a in (*rows, *cols)]
    return pl.pallas_call(
        sum_body,
        out_shape=jax.ShapeDtypeStruct((3, BLK), jnp.float32),
        in_specs=[SMEM] + [VMEM] * 8,
        out_specs=VMEM,
        name="sum_forces",
    )(tab, *args)


def up1_body(m0, m1, m2, m3, tile, embed, w1, w2, w_in, feat_o, sig_o, mixed_o):
    message = (m0[...] + m1[...]) + (m2[...] + m3[...])
    act, sig = ssp_sig(hdot(message, w1[0]))
    feats = feature_rows(tile[...], embed[...]) + hdot(act, w2[0])
    feat_o[...] = feats
    sig_o[...] = sig
    mixed_o[...] = hdot(feats, w_in[1])


def up2_body(m0, m1, m2, m3, feat, w1, w2, wo1, wo2, en_o, gfeat_o, gmsg_o):
    message = (m0[...] + m1[...]) + (m2[...] + m3[...])
    act, sig = ssp_sig(hdot(message, w1[1]))
    feats = feat[...] + hdot(act, w2[1])
    head, head_sig = ssp_sig(hdot(feats, wo1[...]))
    en_o[...] = hdot_t(jnp.broadcast_to(wo2[...], (8, wo2.shape[1])), head)[:1]
    gfeat = hdot_t(head_sig * wo2[...], wo1[...])
    gfeat_o[...] = gfeat
    gmsg_o[...] = hdot_t(hdot_t(gfeat, w2[1]) * sig, w1[1])


def up3_body(m0, m1, m2, m3, gfeat, sig, w_in, w1, w2, gmsg_o):
    total = (m0[...] + m1[...]) + (m2[...] + m3[...])
    gf = gfeat[...] + hdot_t(total, w_in[1])
    gmsg_o[...] = hdot_t(hdot_t(gf, w2[0]) * sig[...], w1[0])


X_SHIFT = {k: [(i, ((i // 4 + k) % 4) * 4 + i % 4) for i in range(16)] for k in (1, 2, 3)}
Y_SHIFT = {k: [(i, (i // 4) * 4 + (i + k) % 4) for i in range(8)] for k in (1, 2, 3)}
CORE = [(i, i ^ 1) for i in range(16)]
Z_LO = [(i, i ^ 2) for i in range(16)]
Z_HI = [(i, i ^ 4) for i in range(8)]


def by_x(v):
    return [lax.ppermute(v, "col", X_SHIFT[k]) for k in (1, 2, 3)]


def by_y(v):
    return [lax.ppermute(v, "row", Y_SHIFT[k]) for k in (1, 2, 3)]


def core(v):
    return lax.ppermute(v, "col", CORE)


def z_lo(v):
    return lax.ppermute(v, "col", Z_LO)


def z_hi(v):
    return lax.ppermute(v, "row", Z_HI)


def coords(t):
    return t // 4, (t // 2) % 2, t % 2


def own_table(own):
    mx, mzl, mco = coords(lax.axis_index("col"))
    mz, my = lax.axis_index("row") // 4, lax.axis_index("row") % 4
    a, b, live = own[:, 0], own[:, 1], own[:, 2]
    tx, tz, tc = coords(a)
    row_idx = ((mx - tx) % 4) * 4 + (tz ^ mzl) * 2 + (tc ^ mco)
    col_idx = ((my - b % 4) % 4) * 2 + ((b // 4) ^ mz)
    return jnp.concatenate([row_idx, col_idx, live])


def index_table(own_part, lists_c, lists_r):
    q, r = lax.axis_index("col"), lax.axis_index("row")
    mx, mzl, mco = coords(q)
    mz, my = r // 4, r % 4
    a, b = lists_c[0, :, 0], lists_c[0, :, 1]
    tx, tz, tc = coords(a)
    agc = jnp.where(tz == mzl, (mx - tx) % 4 + 4 * (tc ^ mco), 8 + jnp.arange(2))
    agr = jnp.where(b // 4 == mz, (my - b % 4) % 4, 4 + jnp.arange(2))
    near_c = lists_c.reshape(2, 2, 2, 3).transpose(1, 0, 2, 3).reshape(8, 3)
    nx, nz, nc = coords(near_c[:, 0])
    rsc = jnp.where((near_c[:, 2] == 1) & (nz == mzl) & (nc == mco), (nx - mx) % 4, -1)
    near_r = lists_r.reshape(4, 3)
    rsr = jnp.where(
        (near_r[:, 2] == 1) & (near_r[:, 1] // 4 == mz), (near_r[:, 1] % 4 - my) % 4, -1
    )
    px, pz, pc = coords(lists_c[2][:, 0])
    agcs = jnp.where(pz == mzl, (mx - px) % 4 + 4 * (pc ^ mco), 0)
    pb = lists_r[1][:, 1]
    agrs = jnp.where(pb // 4 == mz, (my - pb % 4) % 4, 0)
    return jnp.concatenate([own_part, rsc, rsr, agc, agcs, agr, agrs])


def final_table(lists_c, lists_r):
    flat_c = lists_c.reshape(4, 2, 2, 2, 3).transpose(0, 2, 1, 3, 4).reshape(32, 3)
    wrow = (flat_c[:, 2] == 1) & (flat_c[:, 0] == lax.axis_index("col"))
    flat_r = lists_r.reshape(16, 3)
    wcol = (flat_r[:, 2] == 1) & (flat_r[:, 1] == lax.axis_index("row"))
    return jnp.concatenate([wrow, wcol]).astype(jnp.int32)


def body(
    positions,
    species,
    tile_list,
    pair_mask,
    embed,
    w_in,
    rbf_weight,
    rbf_bias,
    filt_weight,
    w_update1,
    w_update2,
    w_out1,
    w_out2,
):
    f32 = jnp.float32
    lists = jnp.pad(tile_list.reshape(1, 6).astype(f32), ((0, 0), (0, BLK - 6)))
    tile = jnp.concatenate(
        [positions, species.astype(f32)[None], lists, jnp.zeros((3, BLK), f32)], axis=0
    )
    far, high = lax.optimization_barrier((core(tile), z_hi(tile)))
    c2 = jnp.stack([tile, far])
    r2 = jnp.stack([tile, high])
    far, high = lax.optimization_barrier((z_lo(c2), by_y(r2)))
    c4 = jnp.concatenate([c2, far])
    c16 = jnp.concatenate([c4] + by_x(c4))
    r8 = jnp.concatenate([r2] + high)
    own_part = own_table(tile_list.reshape(2, 3))

    def lists_of(tiles):
        return tiles[:, 4, :6].astype(jnp.int32).reshape(tiles.shape[0], 2, 3)

    tab = index_table(own_part, lists_of(c4), lists_of(r2))
    masks = pair_mask.reshape(2, BLK, BLK)
    block = near(BLK, BLK)

    def gather_rows(v):
        four = [v] + by_x(v)
        return four, core(jnp.stack(four))

    def reduce_rows(m, name):
        m, far = lax.optimization_barrier((m, z_lo(m)))
        parts = combine_call(tab, [m, far, core(m), core(far)], T_RSC, name)
        return [parts[0]] + [lax.ppermute(parts[k], "col", X_SHIFT[k]) for k in (1, 2, 3)]

    m0, feat0, xm, fil1, q0, q1 = filter_call(
        own_part, c16, r8, masks, embed, w_in, rbf_weight, rbf_bias, filt_weight
    )
    parts = reduce_rows(m0, "combine0")
    own_feat, sig0, mixed1 = call(
        up1_body,
        [block] * 3,
        None,
        [*parts, tile],
        [embed, w_update1, w_update2, w_in],
        name="update0",
    )
    four = [mixed1] + by_y(mixed1)
    sent = z_hi(select_call(tab, four, T_AGRS, "select_x"))
    m1, feat1 = call(
        msg1_body, [near(2, BLK, BLK)] * 2, tab, [*four, sent], store=fil1, name="msg1"
    )
    parts = reduce_rows(m1, "combine1")
    energy, gfeat2, gmsg1 = call(
        up2_body,
        [jax.ShapeDtypeStruct((1, BLK), f32), block, block],
        None,
        [*parts, own_feat],
        [w_update1, w_update2, w_out1, w_out2[None]],
        name="update1",
    )
    tiles_c, tiles_r, gmsg1 = lax.optimization_barrier((c16, r8, gmsg1))
    tab_f = final_table(lists_of(tiles_c), lists_of(tiles_r))
    four, other = gather_rows(gmsg1)
    sent = z_lo(select_call(tab, [*four, other], T_AGCS, "select_g1"))
    dfeat, grad1 = call(
        dfeat_body, [near(2, BLK, BLK)] * 2, tab, [*four, other, sent], store=fil1, name="dfeat"
    )

    def slope1(slot):
        return call(
            lambda *refs: slope1_body(*refs, slot=slot),
            [block],
            None,
            [grad1, feat1],
            store=q1,
            rows=(slot * BLK, slot * BLK + BLK // 2),
            scratch=[pltpu.VMEM((2, BLK, BLK), jnp.bfloat16), pltpu.VMEM((2, BLK, BLK), f32)],
            name=f"slope1_{slot}",
        )[0]

    far, first0 = lax.optimization_barrier((z_hi(dfeat), slope1(0)))
    parts = combine_call(tab, [dfeat, far], T_RSR, "combine_d")
    parts = [parts[0]] + [lax.ppermute(parts[k], "row", Y_SHIFT[k]) for k in (1, 2, 3)]
    (gmsg0,) = call(
        up3_body,
        [block],
        None,
        [*parts, gfeat2, sig0],
        [w_in, w_update1, w_update2],
        name="update2",
    )
    four, other = gather_rows(gmsg0)
    sent = z_lo(select_call(tab, [*four, other], T_AGCS, "select_g0"))
    sent, first1 = lax.optimization_barrier((sent, slope1(1)))
    rf, cf = call(
        force_body,
        [near(2, 8, BLK)] * 2,
        tab,
        [c16, r8, xm, first0, first1, *four, other, sent],
        store=q0,
        scratch=[pltpu.VMEM((2, BLK, BLK), f32)] * 2 + [pltpu.VMEM((2, BLK, BLK), jnp.bfloat16)],
        name="force",
    )
    far, high = lax.optimization_barrier((z_lo(rf), z_hi(cf)))
    rf4 = jnp.concatenate([rf, far])
    cf4 = jnp.concatenate([cf, high])
    far, high = lax.optimization_barrier((core(rf4), by_y(cf4)))
    rf8 = jnp.concatenate([rf4, far])
    forces = sum_call(tab_f, [rf8] + by_x(rf8), [cf4] + high)
    return (energy.reshape(BLK), forces)


def solution(mesh):
    return jax.shard_map(
        body,
        mesh=mesh,
        in_specs=(
            P(None, ("row", "col")),
            P(("row", "col")),
            P("row", "col", None, None),
            P("row", "col", None, None, None),
            P(),
            P(),
            P(),
            P(),
            P(),
            P(),
            P(),
            P(),
            P(),
        ),
        out_specs=(P(("row", "col")), P(None, ("row", "col"))),
        check_vma=False,
    )
```

```python
import math

import jax
import jax.numpy as jnp
from jax import lax
from jax.experimental import pallas as pl
from jax.experimental.pallas import tpu as pltpu
from jax.sharding import PartitionSpec as P

BLK = 128
GAUSS = 256
CUTOFF = 5.0
NORM_DIV = 4.0
STEP = CUTOFF / GAUSS
LN2 = math.log(2.0)
LOG2E = 1.0 / LN2
ALPHA = math.sqrt(LOG2E / 32.0)
SLOPE = -2.0 * LN2 * ALPHA / STEP
HIGH = lax.Precision.HIGHEST
GRP = 8
SUB = 4


SMEM = pl.BlockSpec(memory_space=pltpu.SMEM)
VMEM = pl.BlockSpec(memory_space=pltpu.VMEM)


def near(*shape, dtype=jnp.float32):
    return pltpu.VMEM(shape, dtype)


HBM = pl.BlockSpec(memory_space=pltpu.HBM)
CHUNKS = 8
ROWS = 2 * BLK // CHUNKS
STORE = (2 * BLK, BLK, BLK)


def call(fn, outs, tab, args, weights=(), store=None, rows=(0, BLK), scratch=(), name=None):
    args = [pltpu.with_memory_space_constraint(a, pltpu.VMEM) for a in args]
    held = list(weights) + ([] if store is None else [store])
    held = [pltpu.with_memory_space_constraint(a, pltpu.HBM) for a in held]
    tabs = [] if tab is None else [tab]
    n_in, n_w, n_h, n_out = len(tabs) + len(args), len(weights), len(held), len(outs)

    def kernel(*refs):
        ins, far = refs[:n_in], refs[n_in : n_in + n_h]
        out = refs[n_in + n_h : n_in + n_h + n_out]
        rest = refs[n_in + n_h + n_out :]
        local, sems, extra = rest[:n_h], rest[n_h], rest[n_h + 1 :]
        copies = [pltpu.make_async_copy(far[n], local[n], sems.at[n]) for n in range(n_w)]
        for copy in copies:
            copy.start()
        feed = []
        if store is not None:

            def chunk(n):
                at = pl.ds(n * ROWS, ROWS)
                return pltpu.make_async_copy(far[-1].at[at], local[-1].at[at], sems.at[n_w + n])

            for n in range((rows[1] - rows[0]) // ROWS):
                for row in rows:
                    chunk(row // ROWS + n).start()
            feed = [lambda step: stream(step, chunk, rows)]
        for copy in copies:
            copy.wait()
        fn(*ins, *local, *out, *extra, *feed)

    return pl.pallas_call(
        kernel,
        out_shape=list(outs),
        in_specs=[SMEM] * len(tabs) + [VMEM] * len(args) + [HBM] * n_h,
        out_specs=[HBM if getattr(o, "memory_space", None) == pltpu.HBM else VMEM for o in outs],
        scratch_shapes=[pltpu.VMEM(a.shape, a.dtype) for a in held]
        + [pltpu.SemaphoreType.DMA((max(n_w + (CHUNKS if store is not None else 0), 1),))]
        + list(scratch),
        compiler_params=pltpu.CompilerParams(vmem_limit_bytes=24 << 20),
        name=name,
    )(*tabs, *args, *held)


def stream(fn, chunk, rows):
    per = ROWS // GRP

    def step(it, carry):
        @pl.when(lax.rem(it, per) == 0)
        def _():
            for row in rows:
                chunk(row // ROWS + it // per).wait()

        for half, row in enumerate(rows):
            fn(row // BLK, pl.multiple_of(row % BLK + it * GRP, GRP), half)
        return carry

    lax.fori_loop(0, (rows[1] - rows[0]) // GRP, step, 0)


def hdot(a, b):
    return jnp.dot(a, b, precision=HIGH, preferred_element_type=jnp.float32)


def hdot_t(a, b):
    return lax.dot_general(
        a, b, (((1,), (1,)), ((), ())), precision=HIGH, preferred_element_type=jnp.float32
    )


def ssp_sig(v):
    e = jnp.exp(-jnp.abs(v))
    act = jnp.maximum(v, 0.0) + jnp.log(1.0 + e) - LN2
    sig = jnp.where(v >= 0.0, 1.0, e) / (1.0 + e)
    return act, sig


SLOT = 3
ROW_LISTS = 2 + 4 * 2 * SLOT
CAND = (0, 2, 1, 3)


def coords(t):
    return t >> 2, (t >> 1) & 1, t & 1


def entry(info, base, dev, s):
    at = base + (dev * 2 + s) * SLOT
    return info[at], info[at + 1], info[at + 2]


def row_index(info, s):
    (mx, mz, mc), (x, z, c) = coords(info[0]), coords(entry(info, 2, 0, s)[0])
    return ((mx - x) & 3) * 4 + (z ^ mz) * 2 + (c ^ mc)


def col_index(info, s):
    r, b = info[1], entry(info, 2, 0, s)[1]
    return ((r - b) & 3) * 2 + ((b >> 2) ^ (r >> 2))


def row_block(info, s, dev, other):
    (mx, mz, mc), (x, z, c) = coords(info[0]), coords(entry(info, 2, dev, s)[0])
    return jnp.where(z == mz, ((mx - x) & 3) + 4 * (c ^ mc), other)


def col_block(info, s, dev, other):
    r, b = info[1], entry(info, ROW_LISTS, dev, s)[1]
    return jnp.where((b >> 2) == (r >> 2), (r - b) & 3, other)


def need_row(info, s):
    return row_block(info, s, 0, 8 + s)


def send_row(info, s):
    return row_block(info, s, 2, 0)


def need_col(info, s):
    return col_block(info, s, 0, 4 + s)


def send_col(info, s):
    return col_block(info, s, 1, 0)


def into_row(info, n):
    a, _, live = entry(info, 2, CAND[n // 2], n % 2)
    (mx, mz, mc), (x, z, c) = coords(info[0]), coords(a)
    return jnp.where((live == 1) & (z == mz) & (c == mc), (x - mx) & 3, -1)


def into_col(info, n):
    _, b, live = entry(info, ROW_LISTS, n // 2, n % 2)
    r = info[1]
    return jnp.where((live == 1) & ((b >> 2) == (r >> 2)), (b - r) & 3, -1)


def feature_rows(tile, embed):
    spec = jnp.transpose(tile)[:, 3:4]
    kinds = lax.broadcasted_iota(jnp.int32, (BLK, embed.shape[0]), 1).astype(jnp.float32)
    onehot = jnp.where(spec == kinds, 1.0, 0.0)
    return hdot(onehot, embed)


def turn(mat, base):
    return pltpu.roll(mat, lax.rem(BLK - base, BLK), axis=1)


def spread(turned, ks, width):
    return jnp.concatenate(
        [jnp.broadcast_to(turned[:, k : k + 1], (BLK, width)) for k in ks], axis=0
    )


def filter_body(
    tab, c16, r8, mask, embed, w_in, w_rbf, b_rbf, w_fil, m_o, feat_o, x_o, fil_o, q0_o, q1_o,
    cm_s, dcm_s, w_s, f_s, buf_s, out_sem,
):
    for s in range(2):
        rt = c16[row_index(tab, s)]
        ct = r8[col_index(tab, s)]
        ctt = jnp.transpose(ct)
        d2 = jnp.zeros((BLK, BLK), jnp.float32)
        for a in range(3):
            off = rt[a : a + 1, :] - ctt[:, a : a + 1]
            d2 = d2 + off * off
        d = jnp.sqrt(d2 + 0.01)
        live = entry(tab, 2, 0, s)[2].astype(jnp.float32) * (LN2 / NORM_DIV)
        gate = jnp.transpose(mask[s].astype(jnp.float32)) * live
        ang = d * (math.pi / CUTOFF)
        near_by = d < CUTOFF
        x_o[s] = d * (ALPHA / STEP)
        cm_s[s] = jnp.where(near_by, 0.5 * (jnp.cos(ang) + 1.0), 0.0) * gate
        dcm_s[s] = jnp.where(near_by, (-0.5 * math.pi / CUTOFF) * jnp.sin(ang), 0.0) * gate
        feat_o[s] = hdot(feature_rows(ct, embed[...]), w_in[0])
    w_s[:, :BLK] = w_rbf[0]
    w_s[:, BLK:] = w_rbf[1]
    f_s[...] = jnp.zeros_like(f_s)
    f_s[:BLK, :BLK] = w_fil[0]
    f_s[BLK:, BLK:] = w_fil[1]
    stores = (fil_o, q0_o, q1_o)

    def save(it, n):
        slot = lax.rem(it, 2)
        return pltpu.make_async_copy(
            buf_s.at[slot, n], stores[n].at[pl.ds(it * GRP, GRP)], out_sem.at[slot, n]
        )

    def step(it, _):
        s, base = place(it)
        slot = lax.rem(it, 2)

        @pl.when(it >= 2)
        def _():
            for n in range(3):
                save(it - 2, n).wait()

        xt, ct, dt = turn(x_o[s], base), turn(cm_s[s], base), turn(dcm_s[s], base)
        feats = feat_o[s]
        ticks = lax.broadcasted_iota(jnp.int32, (1, GAUSS), 1).astype(jnp.float32) * ALPHA
        bias = jnp.concatenate([b_rbf[0:1], b_rbf[1:2]], axis=1) * LOG2E - 1.0
        rows = []
        for first in range(0, GRP, SUB):
            ks = range(first, first + SUB)
            u = spread(xt, ks, GAUSS) - ticks
            ex = jnp.exp2(math.log2(LOG2E) - u * u)
            pre = jnp.dot(ex.astype(jnp.bfloat16), w_s[...], preferred_element_type=jnp.float32)
            dpre = jnp.dot(
                (u * ex).astype(jnp.bfloat16), w_s[...], preferred_element_type=jnp.float32
            )
            c = spread(ct, ks, BLK)
            cd = c * (SLOPE / (LN2 * LOG2E))
            dc = spread(dt, ks, BLK)
            p2 = pre + bias
            hid = jnp.log2(0.5 + jnp.exp2(p2))
            dhid = jnp.exp2(p2 - hid) * dpre
            mix = jnp.concatenate([dc, dc], axis=1) * hid + jnp.concatenate([cd, cd], axis=1) * dhid
            fil = jnp.dot(hid.astype(jnp.bfloat16), f_s[...], preferred_element_type=jnp.float32)
            slope = jnp.dot(mix.astype(jnp.bfloat16), f_s[...], preferred_element_type=jnp.float32)
            fil0, fil1 = fil[:, :BLK] * c, fil[:, BLK:] * c
            for k in range(SUB):
                here = slice(k * BLK, (k + 1) * BLK)
                rows.append(jnp.sum(fil0[here] * feats, axis=0, keepdims=True))
            at = pl.ds(first, SUB)
            shape = (SUB, BLK, BLK)
            buf_s[slot, 0, at] = fil1.astype(jnp.bfloat16).reshape(shape)
            buf_s[slot, 1, at] = (slope[:, :BLK].reshape(shape) * feats[None]).astype(jnp.bfloat16)
            buf_s[slot, 2, at] = slope[:, BLK:].astype(jnp.bfloat16).reshape(shape)
        m_o[s, pl.ds(base, GRP), :] = jnp.concatenate(rows, axis=0)
        for n in range(3):
            save(it, n).start()
        return 0

    steps = 2 * BLK // GRP
    lax.fori_loop(0, steps, step, 0)
    for it in (steps - 2, steps - 1):
        for n in range(3):
            save(it, n).wait()


def filter_call(tab, c16, r8, mask, embed, w_in, w_rbf, b_rbf, w_fil):
    big = pltpu.HBM(STORE, jnp.bfloat16)
    return call(
        filter_body,
        [near(2, BLK, BLK)] * 3 + [big] * 3,
        tab,
        [c16, r8],
        [mask, embed, w_in, w_rbf, b_rbf, w_fil],
        scratch=[pltpu.VMEM((2, BLK, BLK), jnp.float32)] * 2
        + [
            pltpu.VMEM((GAUSS, 2 * BLK), jnp.bfloat16),
            pltpu.VMEM((2 * BLK, 2 * BLK), jnp.bfloat16),
            pltpu.VMEM((2, 3, GRP, BLK, BLK), jnp.bfloat16),
            pltpu.SemaphoreType.DMA((2, 3)),
        ],
        name="filters",
    )


def pick(code, sources, store):
    for n, read in enumerate(sources):

        @pl.when(code == n)
        def _(read=read):
            store(read())


def readers(refs):
    out = []
    for ref in refs:
        if len(ref.shape) == 2:
            out.append(lambda ref=ref: ref[...])
        else:
            out.extend([lambda ref=ref, n=n: ref[n] for n in range(ref.shape[0])])
    return out


def select_body(tab, *refs, at):
    sources, o = readers(refs[:-1]), refs[-1]
    for s in range(2):

        def store(v, s=s):
            o[s] = v

        pick(at(tab, s), sources, store)


def select_call(tab, blocks, at, name):
    return call(
        lambda *refs: select_body(*refs, at=at), [near(2, BLK, BLK)], tab, blocks, name=name
    )[0]


def combine_body(tab, *refs, at):
    sources, outs = readers(refs[:-4]), refs[-4:]
    for o in outs:
        o[...] = jnp.zeros_like(o)
    for n, read in enumerate(sources):
        goal = at(tab, n)
        for k, o in enumerate(outs):

            @pl.when(goal == k)
            def _(read=read, o=o):
                o[...] += read()


def combine_call(tab, blocks, at, name):
    return call(
        lambda *refs: combine_body(*refs, at=at), [near(BLK, BLK)] * 4, tab, blocks, name=name
    )


def resolve(tab, at, refs, scratch):
    sources = readers(refs)
    for s in range(2):

        def store(v, s=s):
            scratch[s] = v

        pick(at(tab, s), sources, store)


def place(it):
    return it // (BLK // GRP), pl.multiple_of(lax.rem(it, BLK // GRP) * GRP, GRP)


def msg1_body(tab, *refs):
    src, fil, o, feat_o, loop = refs[:-4], *refs[-4:]
    resolve(tab, need_col, src, feat_o)

    def step(s, base, half):
        feats = feat_o[s]
        rows = [
            jnp.sum(fil[s * BLK + base + k].astype(jnp.float32) * feats, axis=0, keepdims=True)
            for k in range(GRP)
        ]
        o[s, pl.ds(base, GRP), :] = jnp.concatenate(rows, axis=0)

    loop(step)


def dfeat_body(tab, *refs):
    src, fil, o, grad_o, loop = refs[:-4], *refs[-4:]
    resolve(tab, need_row, src, grad_o)
    o[...] = jnp.zeros_like(o)

    def step(s, base, half):
        rows = grad_o[s, pl.ds(base, GRP), :]
        acc = o[s]
        for k in range(GRP):
            acc = acc + fil[s * BLK + base + k].astype(jnp.float32) * rows[k : k + 1, :]
        o[s] = acc

    loop(step)


def slope_step(s, base, store, turned, feats, o, out):
    lanes = lax.broadcasted_iota(jnp.int32, (BLK, BLK), 1)
    rows = store[pl.ds(s * BLK + base, GRP)]
    if feats is not None:
        rows = rows * feats[s].astype(jnp.bfloat16)[None]
    prod = jnp.dot(
        rows.reshape(GRP * BLK, BLK), turned[s], preferred_element_type=jnp.float32
    )
    acc = o[out]
    for k in range(GRP):
        acc = jnp.where(lanes == base + k, prod[k * BLK : (k + 1) * BLK], acc)
    o[out] = acc


def slope1_body(grads, feats, store, o, turned, acc, loop, *, slot):
    turned[slot] = jnp.transpose(grads[slot]).astype(jnp.bfloat16)
    acc[...] = jnp.zeros_like(acc)
    loop(
        lambda s, base, half: slope_step(s, base, store, turned, feats, acc, half)
    )
    o[...] = acc[0] + acc[1]


def force_body(tab, c16, r8, xm, first0, first1, *refs):
    src, store, rf_o, cf_o, grad_s, acc_s, turned, loop = refs[:-7], *refs[-7:]
    resolve(tab, need_row, src, grad_s)
    acc_s[...] = jnp.zeros_like(acc_s)
    for s in range(2):
        turned[s] = jnp.transpose(grad_s[s]).astype(jnp.bfloat16)
    loop(lambda s, base, half: slope_step(s, base, store, turned, None, acc_s, half))
    for s, first in enumerate((first0, first1)):
        rt = c16[row_index(tab, s)]
        ctt = jnp.transpose(r8[col_index(tab, s)])
        pull = -(first[...] + acc_s[s]) / (xm[s] * (STEP / ALPHA))
        rows, cols = [], []
        for a in range(3):
            comp = pull * (rt[a : a + 1, :] - ctt[:, a : a + 1])
            rows.append(jnp.sum(comp, axis=0, keepdims=True))
            cols.append(jnp.sum(comp, axis=1, keepdims=True))
        rf_o[s] = jnp.concatenate(rows + [jnp.zeros((5, BLK), jnp.float32)], axis=0)
        cols = jnp.concatenate(cols + [jnp.zeros((BLK, BLK - 3), jnp.float32)], axis=1)
        cf_o[s] = -jnp.transpose(cols)[:8]


def sum_body(info, *refs):
    rows, cols, o = refs[:4], refs[4:8], refs[8]
    acc = jnp.zeros((8, BLK), jnp.float32)
    for n in range(32):
        dev = n // 8 * 4 + CAND[n // 2 % 4]
        a, _, live = entry(info, 2, dev, n % 2)
        acc = acc + rows[n // 8][n % 8] * jnp.where(a == info[0], live, 0).astype(jnp.float32)
    for n in range(16):
        _, b, live = entry(info, 2 + 16 * 2 * SLOT, n // 2, n % 2)
        acc = acc + cols[n // 4][n % 4] * jnp.where(b == info[1], live, 0).astype(jnp.float32)
    o[...] = acc[:3]


def sum_call(tab, rows, cols):
    args = [pltpu.with_memory_space_constraint(a, pltpu.VMEM) for a in (*rows, *cols)]
    return pl.pallas_call(
        sum_body,
        out_shape=jax.ShapeDtypeStruct((3, BLK), jnp.float32),
        in_specs=[SMEM] + [VMEM] * 8,
        out_specs=VMEM,
        name="sum_forces",
    )(tab, *args)


def up1_body(m0, m1, m2, m3, tile, embed, w1, w2, w_in, feat_o, sig_o, mixed_o):
    message = (m0[...] + m1[...]) + (m2[...] + m3[...])
    act, sig = ssp_sig(hdot(message, w1[0]))
    feats = feature_rows(tile[...], embed[...]) + hdot(act, w2[0])
    feat_o[...] = feats
    sig_o[...] = sig
    mixed_o[...] = hdot(feats, w_in[1])


def up2_body(m0, m1, m2, m3, feat, w1, w2, wo1, wo2, en_o, gfeat_o, gmsg_o):
    message = (m0[...] + m1[...]) + (m2[...] + m3[...])
    act, sig = ssp_sig(hdot(message, w1[1]))
    feats = feat[...] + hdot(act, w2[1])
    head, head_sig = ssp_sig(hdot(feats, wo1[...]))
    en_o[...] = hdot_t(jnp.broadcast_to(wo2[...], (8, wo2.shape[1])), head)[:1]
    gfeat = hdot_t(head_sig * wo2[...], wo1[...])
    gfeat_o[...] = gfeat
    gmsg_o[...] = hdot_t(hdot_t(gfeat, w2[1]) * sig, w1[1])


def up3_body(m0, m1, m2, m3, gfeat, sig, w_in, w1, w2, gmsg_o):
    total = (m0[...] + m1[...]) + (m2[...] + m3[...])
    gf = gfeat[...] + hdot_t(total, w_in[1])
    gmsg_o[...] = hdot_t(hdot_t(gf, w2[0]) * sig[...], w1[0])


X_SHIFT = {k: [(i, ((i // 4 + k) % 4) * 4 + i % 4) for i in range(16)] for k in (1, 2, 3)}
Y_SHIFT = {k: [(i, (i // 4) * 4 + (i + k) % 4) for i in range(8)] for k in (1, 2, 3)}
CORE = [(i, i ^ 1) for i in range(16)]
Z_LO = [(i, i ^ 2) for i in range(16)]
Z_HI = [(i, i ^ 4) for i in range(8)]


def by_x(v):
    return [lax.ppermute(v, "col", X_SHIFT[k]) for k in (1, 2, 3)]


def by_y(v):
    return [lax.ppermute(v, "row", Y_SHIFT[k]) for k in (1, 2, 3)]


def core(v):
    return lax.ppermute(v, "col", CORE)


def z_lo(v):
    return lax.ppermute(v, "col", Z_LO)


def z_hi(v):
    return lax.ppermute(v, "row", Z_HI)


def body(
    positions,
    species,
    tile_list,
    pair_mask,
    embed,
    w_in,
    rbf_weight,
    rbf_bias,
    filt_weight,
    w_update1,
    w_update2,
    w_out1,
    w_out2,
):
    f32 = jnp.float32
    lists = jnp.pad(tile_list.reshape(1, 6).astype(f32), ((0, 0), (0, BLK - 6)))
    tile = jnp.concatenate(
        [positions, species.astype(f32)[None], lists, jnp.zeros((3, BLK), f32)], axis=0
    )
    far, high = lax.optimization_barrier((core(tile), z_hi(tile)))
    c2 = jnp.stack([tile, far])
    r2 = jnp.stack([tile, high])
    far, high = lax.optimization_barrier((z_lo(c2), by_y(r2)))
    c4 = jnp.concatenate([c2, far])
    c16 = jnp.concatenate([c4] + by_x(c4))
    r8 = jnp.concatenate([r2] + high)
    place_of = jnp.stack([lax.axis_index("col"), lax.axis_index("row")])

    def info_of(tiles_c, tiles_r):
        flat = [t[:, 4, : 2 * SLOT].astype(jnp.int32).reshape(-1) for t in (tiles_c, tiles_r)]
        return jnp.concatenate([place_of] + flat)

    tab = info_of(c4, r2)
    masks = pair_mask.reshape(2, BLK, BLK)
    block = near(BLK, BLK)

    def gather_rows(v):
        four = [v] + by_x(v)
        return four, core(jnp.stack(four))

    def reduce_rows(m, name):
        m, far = lax.optimization_barrier((m, z_lo(m)))
        parts = combine_call(tab, [m, far, core(m), core(far)], into_row, name)
        return [parts[0]] + [lax.ppermute(parts[k], "col", X_SHIFT[k]) for k in (1, 2, 3)]

    m0, feat0, xm, fil1, q0, q1 = filter_call(
        tab, c16, r8, masks, embed, w_in, rbf_weight, rbf_bias, filt_weight
    )
    parts = reduce_rows(m0, "combine0")
    own_feat, sig0, mixed1 = call(
        up1_body,
        [block] * 3,
        None,
        [*parts, tile],
        [embed, w_update1, w_update2, w_in],
        name="update0",
    )
    four = [mixed1] + by_y(mixed1)
    sent = z_hi(select_call(tab, four, send_col, "select_x"))
    m1, feat1 = call(
        msg1_body, [near(2, BLK, BLK)] * 2, tab, [*four, sent], store=fil1, name="msg1"
    )
    parts = reduce_rows(m1, "combine1")
    energy, gfeat2, gmsg1 = call(
        up2_body,
        [jax.ShapeDtypeStruct((1, BLK), f32), block, block],
        None,
        [*parts, own_feat],
        [w_update1, w_update2, w_out1, w_out2[None]],
        name="update1",
    )
    tiles_c, tiles_r, gmsg1 = lax.optimization_barrier((c16, r8, gmsg1))
    tab_f = info_of(tiles_c, tiles_r)
    four, other = gather_rows(gmsg1)
    sent = z_lo(select_call(tab, [*four, other], send_row, "select_g1"))
    dfeat, grad1 = call(
        dfeat_body, [near(2, BLK, BLK)] * 2, tab, [*four, other, sent], store=fil1, name="dfeat"
    )

    def slope1(slot):
        return call(
            lambda *refs: slope1_body(*refs, slot=slot),
            [block],
            None,
            [grad1, feat1],
            store=q1,
            rows=(slot * BLK, slot * BLK + BLK // 2),
            scratch=[pltpu.VMEM((2, BLK, BLK), jnp.bfloat16), pltpu.VMEM((2, BLK, BLK), f32)],
            name=f"slope1_{slot}",
        )[0]

    far, first0 = lax.optimization_barrier((z_hi(dfeat), slope1(0)))
    parts = combine_call(tab, [dfeat, far], into_col, "combine_d")
    parts = [parts[0]] + [lax.ppermute(parts[k], "row", Y_SHIFT[k]) for k in (1, 2, 3)]
    (gmsg0,) = call(
        up3_body,
        [block],
        None,
        [*parts, gfeat2, sig0],
        [w_in, w_update1, w_update2],
        name="update2",
    )
    four, other = gather_rows(gmsg0)
    sent = z_lo(select_call(tab, [*four, other], send_row, "select_g0"))
    sent, first1 = lax.optimization_barrier((sent, slope1(1)))
    rf, cf = call(
        force_body,
        [near(2, 8, BLK)] * 2,
        tab,
        [c16, r8, xm, first0, first1, *four, other, sent],
        store=q0,
        scratch=[pltpu.VMEM((2, BLK, BLK), f32)] * 2 + [pltpu.VMEM((2, BLK, BLK), jnp.bfloat16)],
        name="force",
    )
    far, high = lax.optimization_barrier((z_lo(rf), z_hi(cf)))
    rf4 = jnp.concatenate([rf, far])
    cf4 = jnp.concatenate([cf, high])
    far, high = lax.optimization_barrier((core(rf4), by_y(cf4)))
    rf8 = jnp.concatenate([rf4, far])
    forces = sum_call(tab_f, [rf8] + by_x(rf8), [cf4] + high)
    return (energy.reshape(BLK), forces)


def solution(mesh):
    return jax.shard_map(
        body,
        mesh=mesh,
        in_specs=(
            P(None, ("row", "col")),
            P(("row", "col")),
            P("row", "col", None, None),
            P("row", "col", None, None, None),
            P(),
            P(),
            P(),
            P(),
            P(),
            P(),
            P(),
            P(),
            P(),
        ),
        out_specs=(P(("row", "col")), P(None, ("row", "col"))),
        check_vma=False,
    )
```

```python
import math

import jax
import jax.numpy as jnp
from jax import lax
from jax.experimental import pallas as pl
from jax.experimental.pallas import tpu as pltpu
from jax.sharding import PartitionSpec as P

BLK = 128
GAUSS = 256
CUTOFF = 5.0
NORM_DIV = 4.0
STEP = CUTOFF / GAUSS
LN2 = math.log(2.0)
LOG2E = 1.0 / LN2
ALPHA = math.sqrt(LOG2E / 32.0)
SLOPE = -2.0 * LN2 * ALPHA / STEP
HIGH = lax.Precision.HIGHEST
GRP = 8
SUB = 4


SMEM = pl.BlockSpec(memory_space=pltpu.SMEM)
VMEM = pl.BlockSpec(memory_space=pltpu.VMEM)


def near(*shape, dtype=jnp.float32):
    return pltpu.VMEM(shape, dtype)


HBM = pl.BlockSpec(memory_space=pltpu.HBM)
CHUNKS = 8
ROWS = 2 * BLK // CHUNKS
STORE = (2 * BLK, BLK, BLK)


def call(fn, outs, tab, args, weights=(), store=None, rows=(0, BLK), scratch=(), name=None):
    args = [pltpu.with_memory_space_constraint(a, pltpu.VMEM) for a in args]
    held = list(weights) + ([] if store is None else [store])
    held = [pltpu.with_memory_space_constraint(a, pltpu.HBM) for a in held]
    tabs = [] if tab is None else [tab]
    n_in, n_w, n_h, n_out = len(tabs) + len(args), len(weights), len(held), len(outs)

    def kernel(*refs):
        ins, far = refs[:n_in], refs[n_in : n_in + n_h]
        out = refs[n_in + n_h : n_in + n_h + n_out]
        rest = refs[n_in + n_h + n_out :]
        local, sems, extra = rest[:n_h], rest[n_h], rest[n_h + 1 :]
        copies = [pltpu.make_async_copy(far[n], local[n], sems.at[n]) for n in range(n_w)]
        for copy in copies:
            copy.start()
        feed = []
        if store is not None:

            def chunk(n):
                at = pl.ds(n * ROWS, ROWS)
                return pltpu.make_async_copy(far[-1].at[at], local[-1].at[at], sems.at[n_w + n])

            for n in range((rows[1] - rows[0]) // ROWS):
                for row in rows:
                    chunk(row // ROWS + n).start()
            feed = [lambda step: stream(step, chunk, rows)]
        for copy in copies:
            copy.wait()
        fn(*ins, *local, *out, *extra, *feed)

    return pl.pallas_call(
        kernel,
        out_shape=list(outs),
        in_specs=[SMEM] * len(tabs) + [VMEM] * len(args) + [HBM] * n_h,
        out_specs=[HBM if getattr(o, "memory_space", None) == pltpu.HBM else VMEM for o in outs],
        scratch_shapes=[pltpu.VMEM(a.shape, a.dtype) for a in held]
        + [pltpu.SemaphoreType.DMA((max(n_w + (CHUNKS if store is not None else 0), 1),))]
        + list(scratch),
        compiler_params=pltpu.CompilerParams(vmem_limit_bytes=24 << 20),
        name=name,
    )(*tabs, *args, *held)


def stream(fn, chunk, rows):
    per = ROWS // GRP

    def step(it, carry):
        @pl.when(lax.rem(it, per) == 0)
        def _():
            for row in rows:
                chunk(row // ROWS + it // per).wait()

        for half, row in enumerate(rows):
            fn(row // BLK, pl.multiple_of(row % BLK + it * GRP, GRP), half)
        return carry

    lax.fori_loop(0, (rows[1] - rows[0]) // GRP, step, 0)


def hdot(a, b):
    return jnp.dot(a, b, precision=HIGH, preferred_element_type=jnp.float32)


def hdot_t(a, b):
    return lax.dot_general(
        a, b, (((1,), (1,)), ((), ())), precision=HIGH, preferred_element_type=jnp.float32
    )


def ssp_sig(v):
    e = jnp.exp(-jnp.abs(v))
    act = jnp.maximum(v, 0.0) + jnp.log(1.0 + e) - LN2
    sig = jnp.where(v >= 0.0, 1.0, e) / (1.0 + e)
    return act, sig


SLOT = 3
ROW_LISTS = 2 + 4 * 2 * SLOT
CAND = (0, 2, 1, 3)


def coords(t):
    return t >> 2, (t >> 1) & 1, t & 1


def entry(info, base, dev, s):
    at = base + (dev * 2 + s) * SLOT
    return info[at], info[at + 1], info[at + 2]


def row_index(info, s):
    (mx, mz, mc), (x, z, c) = coords(info[0]), coords(entry(info, 2, 0, s)[0])
    return ((mx - x) & 3) * 4 + (z ^ mz) * 2 + (c ^ mc)


def col_index(info, s):
    r, b = info[1], entry(info, 2, 0, s)[1]
    return ((r - b) & 3) * 2 + ((b >> 2) ^ (r >> 2))


def row_block(info, s, dev, other):
    (mx, mz, mc), (x, z, c) = coords(info[0]), coords(entry(info, 2, dev, s)[0])
    return jnp.where(z == mz, ((mx - x) & 3) + 4 * (c ^ mc), other)


def col_block(info, s, dev, other):
    r, b = info[1], entry(info, ROW_LISTS, dev, s)[1]
    return jnp.where((b >> 2) == (r >> 2), (r - b) & 3, other)


def need_row(info, s):
    return row_block(info, s, 0, 8 + s)


def send_row(info, s):
    return row_block(info, s, 2, 0)


def need_col(info, s):
    return col_block(info, s, 0, 4 + s)


def send_col(info, s):
    return col_block(info, s, 1, 0)


def into_row(info, n):
    a, _, live = entry(info, 2, CAND[n // 2], n % 2)
    (mx, mz, mc), (x, z, c) = coords(info[0]), coords(a)
    return jnp.where((live == 1) & (z == mz) & (c == mc), (x - mx) & 3, -1)


def into_col(info, n):
    _, b, live = entry(info, ROW_LISTS, n // 2, n % 2)
    r = info[1]
    return jnp.where((live == 1) & ((b >> 2) == (r >> 2)), (b - r) & 3, -1)


def feature_rows(tile, embed):
    spec = jnp.transpose(tile)[:, 3:4]
    kinds = lax.broadcasted_iota(jnp.int32, (BLK, embed.shape[0]), 1).astype(jnp.float32)
    onehot = jnp.where(spec == kinds, 1.0, 0.0)
    return hdot(onehot, embed)


def turn(mat, base):
    return pltpu.roll(mat, lax.rem(BLK - base, BLK), axis=1)


def spread(turned, ks, width):
    return jnp.concatenate(
        [jnp.broadcast_to(turned[:, k : k + 1], (BLK, width)) for k in ks], axis=0
    )


def sin_cos(t):
    t2 = t * t
    sin = cos = jnp.zeros_like(t)
    for n in range(7, -1, -1):
        sin = sin * t2 + (-1.0) ** n / math.factorial(2 * n + 1)
        cos = cos * t2 + (-1.0) ** n / math.factorial(2 * n)
    return sin * t, cos


def filter_body(
    tab, c16, r8, mask, embed, w_in, w_rbf, b_rbf, w_fil, m_o, feat_o, x_o, fil_o, q0_o, q1_o,
    cm_s, dcm_s, w_s, f_s, buf_s, out_sem,
):
    for s in range(2):
        rt = c16[row_index(tab, s)]
        ct = r8[col_index(tab, s)]
        ctt = jnp.transpose(ct)
        d2 = jnp.zeros((BLK, BLK), jnp.float32)
        for a in range(3):
            off = rt[a : a + 1, :] - ctt[:, a : a + 1]
            d2 = d2 + off * off
        d = jnp.sqrt(d2 + 0.01)
        live = entry(tab, 2, 0, s)[2].astype(jnp.float32) * (LN2 / NORM_DIV)
        gate = jnp.transpose(mask[s].astype(jnp.float32)) * live
        near_by = d < CUTOFF
        sin, cos = sin_cos(jnp.minimum(d, CUTOFF) * (0.5 * math.pi / CUTOFF))
        x_o[s] = d * (ALPHA / STEP)
        cm_s[s] = jnp.where(near_by, cos * cos, 0.0) * gate
        dcm_s[s] = jnp.where(near_by, (-math.pi / CUTOFF) * (sin * cos), 0.0) * gate
        feat_o[s] = hdot(feature_rows(ct, embed[...]), w_in[0])
    w_s[:, :BLK] = w_rbf[0]
    w_s[:, BLK:] = w_rbf[1]
    f_s[...] = jnp.zeros_like(f_s)
    f_s[:BLK, :BLK] = w_fil[0]
    f_s[BLK:, BLK:] = w_fil[1]
    stores = (fil_o, q0_o, q1_o)

    def save(it, n):
        slot = lax.rem(it, 2)
        return pltpu.make_async_copy(
            buf_s.at[slot, n], stores[n].at[pl.ds(it * GRP, GRP)], out_sem.at[slot, n]
        )

    def step(it, _):
        s, base = place(it)
        slot = lax.rem(it, 2)

        @pl.when(it >= 2)
        def _():
            for n in range(3):
                save(it - 2, n).wait()

        xt, ct, dt = turn(x_o[s], base), turn(cm_s[s], base), turn(dcm_s[s], base)
        feats = feat_o[s]
        ticks = lax.broadcasted_iota(jnp.int32, (1, GAUSS), 1).astype(jnp.float32) * ALPHA
        bias = jnp.concatenate([b_rbf[0:1], b_rbf[1:2]], axis=1) * LOG2E - 1.0
        rows = []
        for first in range(0, GRP, SUB):
            ks = range(first, first + SUB)
            u = spread(xt, ks, GAUSS) - ticks
            ex = jnp.exp2(math.log2(LOG2E) - u * u)
            pre = jnp.dot(ex.astype(jnp.bfloat16), w_s[...], preferred_element_type=jnp.float32)
            dpre = jnp.dot(
                (u * ex).astype(jnp.bfloat16), w_s[...], preferred_element_type=jnp.float32
            )
            c = spread(ct, ks, BLK)
            cd = c * (SLOPE / (LN2 * LOG2E))
            dc = spread(dt, ks, BLK)
            p2 = pre + bias
            hid = jnp.log2(0.5 + jnp.exp2(p2))
            dhid = jnp.exp2(p2 - hid) * dpre
            mix = jnp.concatenate([dc, dc], axis=1) * hid + jnp.concatenate([cd, cd], axis=1) * dhid
            fil = jnp.dot(hid.astype(jnp.bfloat16), f_s[...], preferred_element_type=jnp.float32)
            slope = jnp.dot(mix.astype(jnp.bfloat16), f_s[...], preferred_element_type=jnp.float32)
            fil0, fil1 = fil[:, :BLK] * c, fil[:, BLK:] * c
            for k in range(SUB):
                here = slice(k * BLK, (k + 1) * BLK)
                rows.append(jnp.sum(fil0[here] * feats, axis=0, keepdims=True))
            at = pl.ds(first, SUB)
            shape = (SUB, BLK, BLK)
            buf_s[slot, 0, at] = fil1.astype(jnp.bfloat16).reshape(shape)
            buf_s[slot, 1, at] = (slope[:, :BLK].reshape(shape) * feats[None]).astype(jnp.bfloat16)
            buf_s[slot, 2, at] = slope[:, BLK:].astype(jnp.bfloat16).reshape(shape)
        m_o[s, pl.ds(base, GRP), :] = jnp.concatenate(rows, axis=0)
        for n in range(3):
            save(it, n).start()
        return 0

    steps = 2 * BLK // GRP
    lax.fori_loop(0, steps, step, 0)
    for it in (steps - 2, steps - 1):
        for n in range(3):
            save(it, n).wait()


def filter_call(tab, c16, r8, mask, embed, w_in, w_rbf, b_rbf, w_fil):
    big = pltpu.HBM(STORE, jnp.bfloat16)
    return call(
        filter_body,
        [near(2, BLK, BLK)] * 3 + [big] * 3,
        tab,
        [c16, r8],
        [mask, embed, w_in, w_rbf, b_rbf, w_fil],
        scratch=[pltpu.VMEM((2, BLK, BLK), jnp.float32)] * 2
        + [
            pltpu.VMEM((GAUSS, 2 * BLK), jnp.bfloat16),
            pltpu.VMEM((2 * BLK, 2 * BLK), jnp.bfloat16),
            pltpu.VMEM((2, 3, GRP, BLK, BLK), jnp.bfloat16),
            pltpu.SemaphoreType.DMA((2, 3)),
        ],
        name="filters",
    )


def pick(code, sources, store):
    for n, read in enumerate(sources):

        @pl.when(code == n)
        def _(read=read):
            store(read())


def readers(refs):
    out = []
    for ref in refs:
        if len(ref.shape) == 2:
            out.append(lambda ref=ref: ref[...])
        else:
            out.extend([lambda ref=ref, n=n: ref[n] for n in range(ref.shape[0])])
    return out


def select_body(tab, *refs, at):
    sources, o = readers(refs[:-1]), refs[-1]
    for s in range(2):

        def store(v, s=s):
            o[s] = v

        pick(at(tab, s), sources, store)


def select_call(tab, blocks, at, name):
    return call(
        lambda *refs: select_body(*refs, at=at), [near(2, BLK, BLK)], tab, blocks, name=name
    )[0]


def combine_body(tab, *refs, at):
    sources, outs = readers(refs[:-4]), refs[-4:]
    for o in outs:
        o[...] = jnp.zeros_like(o)
    for n, read in enumerate(sources):
        goal = at(tab, n)
        for k, o in enumerate(outs):

            @pl.when(goal == k)
            def _(read=read, o=o):
                o[...] += read()


def combine_call(tab, blocks, at, name):
    return call(
        lambda *refs: combine_body(*refs, at=at), [near(BLK, BLK)] * 4, tab, blocks, name=name
    )


def resolve(tab, at, refs, scratch):
    sources = readers(refs)
    for s in range(2):

        def store(v, s=s):
            scratch[s] = v

        pick(at(tab, s), sources, store)


def place(it):
    return it // (BLK // GRP), pl.multiple_of(lax.rem(it, BLK // GRP) * GRP, GRP)


def msg1_body(tab, *refs):
    src, fil, o, feat_o, loop = refs[:-4], *refs[-4:]
    resolve(tab, need_col, src, feat_o)

    def step(s, base, half):
        feats = feat_o[s]
        rows = [
            jnp.sum(fil[s * BLK + base + k].astype(jnp.float32) * feats, axis=0, keepdims=True)
            for k in range(GRP)
        ]
        o[s, pl.ds(base, GRP), :] = jnp.concatenate(rows, axis=0)

    loop(step)


def dfeat_body(tab, *refs):
    src, fil, o, grad_o, loop = refs[:-4], *refs[-4:]
    resolve(tab, need_row, src, grad_o)
    o[...] = jnp.zeros_like(o)

    def step(s, base, half):
        rows = grad_o[s, pl.ds(base, GRP), :]
        acc = o[s]
        for k in range(GRP):
            acc = acc + fil[s * BLK + base + k].astype(jnp.float32) * rows[k : k + 1, :]
        o[s] = acc

    loop(step)


def slope_step(s, base, store, turned, feats, o, out):
    lanes = lax.broadcasted_iota(jnp.int32, (BLK, BLK), 1)
    rows = store[pl.ds(s * BLK + base, GRP)]
    if feats is not None:
        rows = rows * feats[s].astype(jnp.bfloat16)[None]
    prod = jnp.dot(
        rows.reshape(GRP * BLK, BLK), turned[s], preferred_element_type=jnp.float32
    )
    acc = o[out]
    for k in range(GRP):
        acc = jnp.where(lanes == base + k, prod[k * BLK : (k + 1) * BLK], acc)
    o[out] = acc


def slope1_body(grads, feats, store, o, turned, acc, loop, *, slot):
    turned[slot] = jnp.transpose(grads[slot]).astype(jnp.bfloat16)
    acc[...] = jnp.zeros_like(acc)
    loop(
        lambda s, base, half: slope_step(s, base, store, turned, feats, acc, half)
    )
    o[...] = acc[0] + acc[1]


def force_body(tab, c16, r8, xm, first0, first1, *refs):
    src, store, rf_o, cf_o, grad_s, acc_s, turned, loop = refs[:-7], *refs[-7:]
    resolve(tab, need_row, src, grad_s)
    acc_s[...] = jnp.zeros_like(acc_s)
    for s in range(2):
        turned[s] = jnp.transpose(grad_s[s]).astype(jnp.bfloat16)
    loop(lambda s, base, half: slope_step(s, base, store, turned, None, acc_s, half))
    for s, first in enumerate((first0, first1)):
        rt = c16[row_index(tab, s)]
        ctt = jnp.transpose(r8[col_index(tab, s)])
        pull = -(first[...] + acc_s[s]) / (xm[s] * (STEP / ALPHA))
        rows, cols = [], []
        for a in range(3):
            comp = pull * (rt[a : a + 1, :] - ctt[:, a : a + 1])
            rows.append(jnp.sum(comp, axis=0, keepdims=True))
            cols.append(jnp.sum(comp, axis=1, keepdims=True))
        rf_o[s] = jnp.concatenate(rows + [jnp.zeros((5, BLK), jnp.float32)], axis=0)
        cols = jnp.concatenate(cols + [jnp.zeros((BLK, BLK - 3), jnp.float32)], axis=1)
        cf_o[s] = -jnp.transpose(cols)[:8]


def sum_body(info, *refs):
    rows, cols, o = refs[:4], refs[4:8], refs[8]
    acc = jnp.zeros((8, BLK), jnp.float32)
    for n in range(32):
        dev = n // 2
        a, _, live = entry(info, 2, dev, n % 2)
        acc = acc + rows[n // 8][n % 8] * jnp.where(a == info[0], live, 0).astype(jnp.float32)
    for n in range(16):
        _, b, live = entry(info, 2 + 16 * 2 * SLOT, n // 2, n % 2)
        acc = acc + cols[n // 4][n % 4] * jnp.where(b == info[1], live, 0).astype(jnp.float32)
    o[...] = acc[:3]


def sum_call(tab, rows, cols):
    args = [pltpu.with_memory_space_constraint(a, pltpu.VMEM) for a in (*rows, *cols)]
    return pl.pallas_call(
        sum_body,
        out_shape=jax.ShapeDtypeStruct((3, BLK), jnp.float32),
        in_specs=[SMEM] + [VMEM] * 8,
        out_specs=VMEM,
        name="sum_forces",
    )(tab, *args)


def up1_body(m0, m1, m2, m3, tile, embed, w1, w2, w_in, feat_o, sig_o, mixed_o):
    message = (m0[...] + m1[...]) + (m2[...] + m3[...])
    act, sig = ssp_sig(hdot(message, w1[0]))
    feats = feature_rows(tile[...], embed[...]) + hdot(act, w2[0])
    feat_o[...] = feats
    sig_o[...] = sig
    mixed_o[...] = hdot(feats, w_in[1])


def up2_body(m0, m1, m2, m3, feat, w1, w2, wo1, wo2, en_o, gfeat_o, gmsg_o):
    message = (m0[...] + m1[...]) + (m2[...] + m3[...])
    act, sig = ssp_sig(hdot(message, w1[1]))
    feats = feat[...] + hdot(act, w2[1])
    head, head_sig = ssp_sig(hdot(feats, wo1[...]))
    en_o[...] = hdot_t(jnp.broadcast_to(wo2[...], (8, wo2.shape[1])), head)[:1]
    gfeat = hdot_t(head_sig * wo2[...], wo1[...])
    gfeat_o[...] = gfeat
    gmsg_o[...] = hdot_t(hdot_t(gfeat, w2[1]) * sig, w1[1])


def up3_body(m0, m1, m2, m3, gfeat, sig, w_in, w1, w2, gmsg_o):
    total = (m0[...] + m1[...]) + (m2[...] + m3[...])
    gf = gfeat[...] + hdot_t(total, w_in[1])
    gmsg_o[...] = hdot_t(hdot_t(gf, w2[0]) * sig[...], w1[0])


X_SHIFT = {k: [(i, ((i // 4 + k) % 4) * 4 + i % 4) for i in range(16)] for k in (1, 2, 3)}
Y_SHIFT = {k: [(i, (i // 4) * 4 + (i + k) % 4) for i in range(8)] for k in (1, 2, 3)}
CORE = [(i, i ^ 1) for i in range(16)]
Z_LO = [(i, i ^ 2) for i in range(16)]
Z_HI = [(i, i ^ 4) for i in range(8)]


def by_x(v):
    return [lax.ppermute(v, "col", X_SHIFT[k]) for k in (1, 2, 3)]


def by_y(v):
    return [lax.ppermute(v, "row", Y_SHIFT[k]) for k in (1, 2, 3)]


def core(v):
    return lax.ppermute(v, "col", CORE)


def z_lo(v):
    return lax.ppermute(v, "col", Z_LO)


def square(v, other):
    moved = [lax.ppermute(v, "col", [(i, i ^ n) for i in range(16)]) for n in (1, 2, 3)]
    return lax.optimization_barrier((moved, other))


def z_hi(v):
    return lax.ppermute(v, "row", Z_HI)


def body(
    positions,
    species,
    tile_list,
    pair_mask,
    embed,
    w_in,
    rbf_weight,
    rbf_bias,
    filt_weight,
    w_update1,
    w_update2,
    w_out1,
    w_out2,
):
    f32 = jnp.float32
    lists = jnp.pad(tile_list.reshape(1, 6).astype(f32), ((0, 0), (0, BLK - 6)))
    tile = jnp.concatenate(
        [positions, species.astype(f32)[None], lists, jnp.zeros((3, BLK), f32)], axis=0
    )
    near_c, near_r = square(tile, z_hi(tile))
    c4, r2 = jnp.stack([tile, *near_c]), jnp.stack([tile, near_r])
    over_x, over_y = lax.optimization_barrier((by_x(c4), by_y(r2)))
    c16 = jnp.concatenate([c4] + over_x)
    r8 = jnp.concatenate([r2] + over_y)
    place_of = jnp.stack([lax.axis_index("col"), lax.axis_index("row")])

    def info_of(tiles_c, tiles_r):
        flat = [t[:, 4, : 2 * SLOT].astype(jnp.int32).reshape(-1) for t in (tiles_c, tiles_r)]
        return jnp.concatenate([place_of] + flat)

    tab = info_of(c4, r2)
    masks = pair_mask.reshape(2, BLK, BLK)
    block = near(BLK, BLK)

    def gather_rows(v):
        four = [v] + by_x(v)
        return four, core(jnp.stack(four))

    def reduce_rows(m, name):
        m, far = lax.optimization_barrier((m, z_lo(m)))
        parts = combine_call(tab, [m, far, core(m), core(far)], into_row, name)
        return [parts[0]] + [lax.ppermute(parts[k], "col", X_SHIFT[k]) for k in (1, 2, 3)]

    m0, feat0, xm, fil1, q0, q1 = filter_call(
        tab, c16, r8, masks, embed, w_in, rbf_weight, rbf_bias, filt_weight
    )
    parts = reduce_rows(m0, "combine0")
    own_feat, sig0, mixed1 = call(
        up1_body,
        [block] * 3,
        None,
        [*parts, tile],
        [embed, w_update1, w_update2, w_in],
        name="update0",
    )
    four = [mixed1] + by_y(mixed1)
    sent = z_hi(select_call(tab, four, send_col, "select_x"))
    m1, feat1 = call(
        msg1_body, [near(2, BLK, BLK)] * 2, tab, [*four, sent], store=fil1, name="msg1"
    )
    parts = reduce_rows(m1, "combine1")
    energy, gfeat2, gmsg1 = call(
        up2_body,
        [jax.ShapeDtypeStruct((1, BLK), f32), block, block],
        None,
        [*parts, own_feat],
        [w_update1, w_update2, w_out1, w_out2[None]],
        name="update1",
    )
    tiles_c, tiles_r, gmsg1 = lax.optimization_barrier((c16, r8, gmsg1))
    tab_f = info_of(tiles_c, tiles_r)
    four, other = gather_rows(gmsg1)
    sent = z_lo(select_call(tab, [*four, other], send_row, "select_g1"))
    dfeat, grad1 = call(
        dfeat_body, [near(2, BLK, BLK)] * 2, tab, [*four, other, sent], store=fil1, name="dfeat"
    )

    def slope1(slot):
        return call(
            lambda *refs: slope1_body(*refs, slot=slot),
            [block],
            None,
            [grad1, feat1],
            store=q1,
            rows=(slot * BLK, slot * BLK + BLK // 2),
            scratch=[pltpu.VMEM((2, BLK, BLK), jnp.bfloat16), pltpu.VMEM((2, BLK, BLK), f32)],
            name=f"slope1_{slot}",
        )[0]

    far, first0 = lax.optimization_barrier((z_hi(dfeat), slope1(0)))
    parts = combine_call(tab, [dfeat, far], into_col, "combine_d")
    parts = [parts[0]] + [lax.ppermute(parts[k], "row", Y_SHIFT[k]) for k in (1, 2, 3)]
    (gmsg0,) = call(
        up3_body,
        [block],
        None,
        [*parts, gfeat2, sig0],
        [w_in, w_update1, w_update2],
        name="update2",
    )
    four, other = gather_rows(gmsg0)
    sent = z_lo(select_call(tab, [*four, other], send_row, "select_g0"))
    sent, first1 = lax.optimization_barrier((sent, slope1(1)))
    rf, cf = call(
        force_body,
        [near(2, 8, BLK)] * 2,
        tab,
        [c16, r8, xm, first0, first1, *four, other, sent],
        store=q0,
        scratch=[pltpu.VMEM((2, BLK, BLK), f32)] * 2 + [pltpu.VMEM((2, BLK, BLK), jnp.bfloat16)],
        name="force",
    )
    near_c, near_r = square(rf, z_hi(cf))
    rf8, cf4 = jnp.concatenate([rf, *near_c]), jnp.concatenate([cf, near_r])
    over_x, over_y = lax.optimization_barrier((by_x(rf8), by_y(cf4)))
    forces = sum_call(tab_f, [rf8, *over_x], [cf4, *over_y])
    return (energy.reshape(BLK), forces)


def solution(mesh):
    return jax.shard_map(
        body,
        mesh=mesh,
        in_specs=(
            P(None, ("row", "col")),
            P(("row", "col")),
            P("row", "col", None, None),
            P("row", "col", None, None, None),
            P(),
            P(),
            P(),
            P(),
            P(),
            P(),
            P(),
            P(),
            P(),
        ),
        out_specs=(P(("row", "col")), P(None, ("row", "col"))),
        check_vma=False,
    )
```

```python
import math

import jax
import jax.numpy as jnp
from jax import lax
from jax.experimental import pallas as pl
from jax.experimental.pallas import tpu as pltpu
from jax.sharding import PartitionSpec as P

BLK = 128
GAUSS = 256
CUTOFF = 5.0
NORM_DIV = 4.0
STEP = CUTOFF / GAUSS
LN2 = math.log(2.0)
LOG2E = 1.0 / LN2
ALPHA = math.sqrt(LOG2E / 32.0)
SLOPE = -2.0 * LN2 * ALPHA / STEP
HIGH = lax.Precision.HIGHEST
GRP = 8
SUB = 4


SMEM = pl.BlockSpec(memory_space=pltpu.SMEM)
VMEM = pl.BlockSpec(memory_space=pltpu.VMEM)


def near(*shape, dtype=jnp.float32):
    return pltpu.VMEM(shape, dtype)


HBM = pl.BlockSpec(memory_space=pltpu.HBM)
CHUNKS = 8
ROWS = 2 * BLK // CHUNKS
STORE = (2 * BLK, BLK, BLK)


def call(fn, outs, tab, args, weights=(), store=None, rows=(0, BLK), scratch=(), name=None):
    args = [pltpu.with_memory_space_constraint(a, pltpu.VMEM) for a in args]
    held = list(weights) + ([] if store is None else [store])
    held = [pltpu.with_memory_space_constraint(a, pltpu.HBM) for a in held]
    tabs = [] if tab is None else [tab]
    n_in, n_w, n_h, n_out = len(tabs) + len(args), len(weights), len(held), len(outs)

    def kernel(*refs):
        ins, far = refs[:n_in], refs[n_in : n_in + n_h]
        out = refs[n_in + n_h : n_in + n_h + n_out]
        rest = refs[n_in + n_h + n_out :]
        local, sems, extra = rest[:n_h], rest[n_h], rest[n_h + 1 :]
        copies = [pltpu.make_async_copy(far[n], local[n], sems.at[n]) for n in range(n_w)]
        for copy in copies:
            copy.start()
        feed = []
        if store is not None:

            def chunk(n):
                at = pl.ds(n * ROWS, ROWS)
                return pltpu.make_async_copy(far[-1].at[at], local[-1].at[at], sems.at[n_w + n])

            for n in range((rows[1] - rows[0]) // ROWS):
                for row in rows:
                    chunk(row // ROWS + n).start()
            feed = [lambda step: stream(step, chunk, rows)]
        for copy in copies:
            copy.wait()
        fn(*ins, *local, *out, *extra, *feed)

    return pl.pallas_call(
        kernel,
        out_shape=list(outs),
        in_specs=[SMEM] * len(tabs) + [VMEM] * len(args) + [HBM] * n_h,
        out_specs=[HBM if getattr(o, "memory_space", None) == pltpu.HBM else VMEM for o in outs],
        scratch_shapes=[pltpu.VMEM(a.shape, a.dtype) for a in held]
        + [pltpu.SemaphoreType.DMA((max(n_w + (CHUNKS if store is not None else 0), 1),))]
        + list(scratch),
        compiler_params=pltpu.CompilerParams(vmem_limit_bytes=24 << 20),
        name=name,
    )(*tabs, *args, *held)


def stream(fn, chunk, rows):
    per = ROWS // GRP

    def step(it, carry):
        @pl.when(lax.rem(it, per) == 0)
        def _():
            for row in rows:
                chunk(row // ROWS + it // per).wait()

        for half, row in enumerate(rows):
            fn(row // BLK, pl.multiple_of(row % BLK + it * GRP, GRP), half)
        return carry

    lax.fori_loop(0, (rows[1] - rows[0]) // GRP, step, 0)


def hdot(a, b):
    return jnp.dot(a, b, precision=HIGH, preferred_element_type=jnp.float32)


def hdot_t(a, b):
    return lax.dot_general(
        a, b, (((1,), (1,)), ((), ())), precision=HIGH, preferred_element_type=jnp.float32
    )


def ssp_sig(v):
    e = jnp.exp(-jnp.abs(v))
    act = jnp.maximum(v, 0.0) + jnp.log(1.0 + e) - LN2
    sig = jnp.where(v >= 0.0, 1.0, e) / (1.0 + e)
    return act, sig


SLOT = 3
ROW_LISTS = 2 + 4 * 2 * SLOT
CAND = (0, 2, 1, 3)


def coords(t):
    return t >> 2, (t >> 1) & 1, t & 1


def entry(info, base, dev, s):
    at = base + (dev * 2 + s) * SLOT
    return info[at], info[at + 1], info[at + 2]


def row_index(info, s):
    (mx, mz, mc), (x, z, c) = coords(info[0]), coords(entry(info, 2, 0, s)[0])
    return ((mx - x) & 3) * 4 + (z ^ mz) * 2 + (c ^ mc)


def col_index(info, s):
    r, b = info[1], entry(info, 2, 0, s)[1]
    return ((r - b) & 3) * 2 + ((b >> 2) ^ (r >> 2))


def row_block(info, s, dev, other):
    (mx, mz, mc), (x, z, c) = coords(info[0]), coords(entry(info, 2, dev, s)[0])
    return jnp.where(z == mz, ((mx - x) & 3) + 4 * (c ^ mc), other)


def col_block(info, s, dev, other):
    r, b = info[1], entry(info, ROW_LISTS, dev, s)[1]
    return jnp.where((b >> 2) == (r >> 2), (r - b) & 3, other)


def need_row(info, s):
    return row_block(info, s, 0, 8 + s)


def send_row(info, s):
    return row_block(info, s, 2, 0)


def need_col(info, s):
    return col_block(info, s, 0, 4 + s)


def send_col(info, s):
    return col_block(info, s, 1, 0)


def into_row(info, n):
    a, _, live = entry(info, 2, CAND[n // 2], n % 2)
    (mx, mz, mc), (x, z, c) = coords(info[0]), coords(a)
    return jnp.where((live == 1) & (z == mz) & (c == mc), (x - mx) & 3, -1)


def into_col(info, n):
    _, b, live = entry(info, ROW_LISTS, n // 2, n % 2)
    r = info[1]
    return jnp.where((live == 1) & ((b >> 2) == (r >> 2)), (b - r) & 3, -1)


def feature_rows(tile, embed):
    spec = jnp.transpose(tile)[:, 3:4]
    kinds = lax.broadcasted_iota(jnp.int32, (BLK, embed.shape[0]), 1).astype(jnp.float32)
    onehot = jnp.where(spec == kinds, 1.0, 0.0)
    return hdot(onehot, embed)


def turn(mat, base):
    return pltpu.roll(mat, lax.rem(BLK - base, BLK), axis=1)


def spread(turned, ks, width):
    return jnp.concatenate(
        [jnp.broadcast_to(turned[:, k : k + 1], (BLK, width)) for k in ks], axis=0
    )


def sin_cos(t):
    t2 = t * t
    sin = cos = jnp.zeros_like(t)
    for n in range(7, -1, -1):
        sin = sin * t2 + (-1.0) ** n / math.factorial(2 * n + 1)
        cos = cos * t2 + (-1.0) ** n / math.factorial(2 * n)
    return sin * t, cos


def filter_body(
    tab, c16, r8, mask, embed, w_in, w_rbf, b_rbf, w_fil, m_o, feat_o, x_o, fil_o, q0_o, q1_o,
    cm_s, dcm_s, w_s, f_s, buf_s, out_sem,
):
    for s in range(2):
        rt = c16[row_index(tab, s)]
        ct = r8[col_index(tab, s)]
        ctt = jnp.transpose(ct)
        d2 = jnp.zeros((BLK, BLK), jnp.float32)
        for a in range(3):
            off = rt[a : a + 1, :] - ctt[:, a : a + 1]
            d2 = d2 + off * off
        d = jnp.sqrt(d2 + 0.01)
        live = entry(tab, 2, 0, s)[2].astype(jnp.float32) * (LN2 / NORM_DIV)
        gate = jnp.transpose(mask[s].astype(jnp.float32)) * live
        near_by = d < CUTOFF
        sin, cos = sin_cos(jnp.minimum(d, CUTOFF) * (0.5 * math.pi / CUTOFF))
        x_o[s] = d * (ALPHA / STEP)
        cm_s[s] = jnp.where(near_by, cos * cos, 0.0) * gate
        dcm_s[s] = jnp.where(near_by, (-math.pi / CUTOFF) * (sin * cos), 0.0) * gate
        feat_o[s] = hdot(feature_rows(ct, embed[...]), w_in[0])
    w_s[:, :BLK] = w_rbf[0]
    w_s[:, BLK:] = w_rbf[1]
    f_s[...] = jnp.zeros_like(f_s)
    f_s[:BLK, :BLK] = w_fil[0]
    f_s[BLK:, BLK:] = w_fil[1]
    stores = (fil_o, q0_o, q1_o)

    def save(it, n):
        slot = lax.rem(it, 2)
        return pltpu.make_async_copy(
            buf_s.at[slot, n], stores[n].at[pl.ds(it * GRP, GRP)], out_sem.at[slot, n]
        )

    def step(it, _):
        s, base = place(it)
        slot = lax.rem(it, 2)

        @pl.when(it >= 2)
        def _():
            for n in range(3):
                save(it - 2, n).wait()

        xt, ct, dt = turn(x_o[s], base), turn(cm_s[s], base), turn(dcm_s[s], base)
        feats = feat_o[s]
        ticks = lax.broadcasted_iota(jnp.int32, (1, GAUSS), 1).astype(jnp.float32) * ALPHA
        bias = jnp.concatenate([b_rbf[0:1], b_rbf[1:2]], axis=1) * LOG2E - 1.0
        rows = []
        for first in range(0, GRP, SUB):
            ks = range(first, first + SUB)
            u = spread(xt, ks, GAUSS) - ticks
            ex = jnp.exp2(math.log2(LOG2E) - u * u)
            pre = jnp.dot(ex.astype(jnp.bfloat16), w_s[...], preferred_element_type=jnp.float32)
            dpre = jnp.dot(
                (u * ex).astype(jnp.bfloat16), w_s[...], preferred_element_type=jnp.float32
            )
            c = spread(ct, ks, BLK)
            cd = c * (SLOPE / (LN2 * LOG2E))
            dc = spread(dt, ks, BLK)
            p2 = pre + bias
            hid = jnp.log2(0.5 + jnp.exp2(p2))
            dhid = jnp.exp2(p2 - hid) * dpre
            mix = jnp.concatenate([dc, dc], axis=1) * hid + jnp.concatenate([cd, cd], axis=1) * dhid
            fil = jnp.dot(hid.astype(jnp.bfloat16), f_s[...], preferred_element_type=jnp.float32)
            slope = jnp.dot(mix.astype(jnp.bfloat16), f_s[...], preferred_element_type=jnp.float32)
            fil0, fil1 = fil[:, :BLK] * c, fil[:, BLK:] * c
            for k in range(SUB):
                here = slice(k * BLK, (k + 1) * BLK)
                rows.append(jnp.sum(fil0[here] * feats, axis=0, keepdims=True))
            at = pl.ds(first, SUB)
            shape = (SUB, BLK, BLK)
            buf_s[slot, 0, at] = fil1.astype(jnp.bfloat16).reshape(shape)
            buf_s[slot, 1, at] = (slope[:, :BLK].reshape(shape) * feats[None]).astype(jnp.bfloat16)
            buf_s[slot, 2, at] = slope[:, BLK:].astype(jnp.bfloat16).reshape(shape)
        m_o[s, pl.ds(base, GRP), :] = jnp.concatenate(rows, axis=0)
        for n in range(3):
            save(it, n).start()
        return 0

    steps = 2 * BLK // GRP
    lax.fori_loop(0, steps, step, 0)
    for it in (steps - 2, steps - 1):
        for n in range(3):
            save(it, n).wait()


def filter_call(tab, c16, r8, mask, embed, w_in, w_rbf, b_rbf, w_fil):
    big = pltpu.HBM(STORE, jnp.bfloat16)
    return call(
        filter_body,
        [near(2, BLK, BLK)] * 3 + [big] * 3,
        tab,
        [c16, r8],
        [mask, embed, w_in, w_rbf, b_rbf, w_fil],
        scratch=[pltpu.VMEM((2, BLK, BLK), jnp.float32)] * 2
        + [
            pltpu.VMEM((GAUSS, 2 * BLK), jnp.bfloat16),
            pltpu.VMEM((2 * BLK, 2 * BLK), jnp.bfloat16),
            pltpu.VMEM((2, 3, GRP, BLK, BLK), jnp.bfloat16),
            pltpu.SemaphoreType.DMA((2, 3)),
        ],
        name="filters",
    )


def pick(code, sources, store):
    for n, read in enumerate(sources):

        @pl.when(code == n)
        def _(read=read):
            store(read())


def readers(refs):
    out = []
    for ref in refs:
        if len(ref.shape) == 2:
            out.append(lambda ref=ref: ref[...])
        else:
            out.extend([lambda ref=ref, n=n: ref[n] for n in range(ref.shape[0])])
    return out


def select_body(tab, *refs, at):
    sources, o = readers(refs[:-1]), refs[-1]
    for s in range(2):

        def store(v, s=s):
            o[s] = v

        pick(at(tab, s), sources, store)


def select_call(tab, blocks, at, name):
    return call(
        lambda *refs: select_body(*refs, at=at), [near(2, BLK, BLK)], tab, blocks, name=name
    )[0]


def combine_body(tab, *refs, at):
    sources, outs = readers(refs[:-4]), refs[-4:]
    for o in outs:
        o[...] = jnp.zeros_like(o)
    for n, read in enumerate(sources):
        goal = at(tab, n)
        for k, o in enumerate(outs):

            @pl.when(goal == k)
            def _(read=read, o=o):
                o[...] += read()


def combine_call(tab, blocks, at, name):
    return call(
        lambda *refs: combine_body(*refs, at=at), [near(BLK, BLK)] * 4, tab, blocks, name=name
    )


def resolve(tab, at, refs, scratch):
    sources = readers(refs)
    for s in range(2):

        def store(v, s=s):
            scratch[s] = v

        pick(at(tab, s), sources, store)


def place(it):
    return it // (BLK // GRP), pl.multiple_of(lax.rem(it, BLK // GRP) * GRP, GRP)


def msg1_body(tab, *refs):
    src, fil, o, feat_o, loop = refs[:-4], *refs[-4:]
    resolve(tab, need_col, src, feat_o)

    def step(s, base, half):
        feats = feat_o[s]
        rows = [
            jnp.sum(fil[s * BLK + base + k].astype(jnp.float32) * feats, axis=0, keepdims=True)
            for k in range(GRP)
        ]
        o[s, pl.ds(base, GRP), :] = jnp.concatenate(rows, axis=0)

    loop(step)


def dfeat_body(tab, *refs):
    src, fil, o, grad_o, loop = refs[:-4], *refs[-4:]
    resolve(tab, need_row, src, grad_o)
    o[...] = jnp.zeros_like(o)

    def step(s, base, half):
        rows = grad_o[s, pl.ds(base, GRP), :]
        acc = o[s]
        for k in range(GRP):
            acc = acc + fil[s * BLK + base + k].astype(jnp.float32) * rows[k : k + 1, :]
        o[s] = acc

    loop(step)


def slope_step(s, base, store, turned, feats, o, out):
    lanes = lax.broadcasted_iota(jnp.int32, (BLK, BLK), 1)
    rows = store[pl.ds(s * BLK + base, GRP)]
    if feats is not None:
        rows = rows * feats[s].astype(jnp.bfloat16)[None]
    prod = jnp.dot(
        rows.reshape(GRP * BLK, BLK), turned[s], preferred_element_type=jnp.float32
    )
    acc = o[out]
    for k in range(GRP):
        acc = jnp.where(lanes == base + k, prod[k * BLK : (k + 1) * BLK], acc)
    o[out] = acc


def slope1_body(grads, feats, store, o, turned, acc, loop, *, slot):
    turned[slot] = jnp.transpose(grads[slot]).astype(jnp.bfloat16)
    acc[...] = jnp.zeros_like(acc)
    loop(
        lambda s, base, half: slope_step(s, base, store, turned, feats, acc, half)
    )
    o[...] = acc[0] + acc[1]


def force_body(tab, c16, r8, xm, first0, first1, *refs):
    src, store, rf_o, cf_o, grad_s, acc_s, turned, loop = refs[:-7], *refs[-7:]
    resolve(tab, need_row, src, grad_s)
    acc_s[...] = jnp.zeros_like(acc_s)
    for s in range(2):
        turned[s] = jnp.transpose(grad_s[s]).astype(jnp.bfloat16)
    loop(lambda s, base, half: slope_step(s, base, store, turned, None, acc_s, half))
    for s, first in enumerate((first0, first1)):
        rt = c16[row_index(tab, s)]
        ctt = jnp.transpose(r8[col_index(tab, s)])
        pull = -(first[...] + acc_s[s]) / (xm[s] * (STEP / ALPHA))
        rows, cols = [], []
        for a in range(3):
            comp = pull * (rt[a : a + 1, :] - ctt[:, a : a + 1])
            rows.append(jnp.sum(comp, axis=0, keepdims=True))
            cols.append(jnp.sum(comp, axis=1, keepdims=True))
        rf_o[s] = jnp.concatenate(rows + [jnp.zeros((5, BLK), jnp.float32)], axis=0)
        cols = jnp.concatenate(cols + [jnp.zeros((BLK, BLK - 3), jnp.float32)], axis=1)
        cf_o[s] = -jnp.transpose(cols)[:8]


def sum_body(info, *refs):
    rows, cols, o = refs[:4], refs[4:8], refs[8]
    acc = jnp.zeros((8, BLK), jnp.float32)
    for n in range(32):
        dev = n // 2
        a, _, live = entry(info, 2, dev, n % 2)
        acc = acc + rows[n // 8][n % 8] * jnp.where(a == info[0], live, 0).astype(jnp.float32)
    for n in range(16):
        _, b, live = entry(info, 2 + 16 * 2 * SLOT, n // 2, n % 2)
        acc = acc + cols[n // 4][n % 4] * jnp.where(b == info[1], live, 0).astype(jnp.float32)
    o[...] = acc[:3]


def sum_call(tab, rows, cols):
    args = [pltpu.with_memory_space_constraint(a, pltpu.VMEM) for a in (*rows, *cols)]
    return pl.pallas_call(
        sum_body,
        out_shape=jax.ShapeDtypeStruct((3, BLK), jnp.float32),
        in_specs=[SMEM] + [VMEM] * 8,
        out_specs=VMEM,
        name="sum_forces",
    )(tab, *args)


def up1_body(m0, m1, m2, m3, tile, embed, w1, w2, w_in, feat_o, sig_o, mixed_o):
    message = (m0[...] + m1[...]) + (m2[...] + m3[...])
    act, sig = ssp_sig(hdot(message, w1[0]))
    feats = feature_rows(tile[...], embed[...]) + hdot(act, w2[0])
    feat_o[...] = feats
    sig_o[...] = sig
    mixed_o[...] = hdot(feats, w_in[1])


def up2_body(m0, m1, m2, m3, feat, w1, w2, wo1, wo2, en_o, gfeat_o, gmsg_o):
    message = (m0[...] + m1[...]) + (m2[...] + m3[...])
    act, sig = ssp_sig(hdot(message, w1[1]))
    feats = feat[...] + hdot(act, w2[1])
    head, head_sig = ssp_sig(hdot(feats, wo1[...]))
    en_o[...] = hdot_t(jnp.broadcast_to(wo2[...], (8, wo2.shape[1])), head)[:1]
    gfeat = hdot_t(head_sig * wo2[...], wo1[...])
    gfeat_o[...] = gfeat
    gmsg_o[...] = hdot_t(hdot_t(gfeat, w2[1]) * sig, w1[1])


def up3_body(m0, m1, m2, m3, gfeat, sig, w_in, w1, w2, gmsg_o):
    total = (m0[...] + m1[...]) + (m2[...] + m3[...])
    gf = gfeat[...] + hdot_t(total, w_in[1])
    gmsg_o[...] = hdot_t(hdot_t(gf, w2[0]) * sig[...], w1[0])


X_SHIFT = {k: [(i, ((i // 4 + k) % 4) * 4 + i % 4) for i in range(16)] for k in (1, 2, 3)}
Y_SHIFT = {k: [(i, (i // 4) * 4 + (i + k) % 4) for i in range(8)] for k in (1, 2, 3)}
CORE = [(i, i ^ 1) for i in range(16)]
Z_LO = [(i, i ^ 2) for i in range(16)]
Z_HI = [(i, i ^ 4) for i in range(8)]


def ring(v, axis, shift):
    behind = lax.ppermute(v, axis, shift[1])
    ahead = lax.ppermute(v, axis, shift[3])
    return [behind, lax.ppermute(behind, axis, shift[1]), ahead]


def by_x(v):
    return ring(v, "col", X_SHIFT)


def by_y(v):
    return ring(v, "row", Y_SHIFT)


def core(v):
    return lax.ppermute(v, "col", CORE)


def z_lo(v):
    return lax.ppermute(v, "col", Z_LO)


def square(v, other):
    moved = [lax.ppermute(v, "col", [(i, i ^ n) for i in range(16)]) for n in (1, 2, 3)]
    return lax.optimization_barrier((moved, other))


def z_hi(v):
    return lax.ppermute(v, "row", Z_HI)


def body(
    positions,
    species,
    tile_list,
    pair_mask,
    embed,
    w_in,
    rbf_weight,
    rbf_bias,
    filt_weight,
    w_update1,
    w_update2,
    w_out1,
    w_out2,
):
    f32 = jnp.float32
    lists = jnp.pad(tile_list.reshape(1, 6).astype(f32), ((0, 0), (0, BLK - 6)))
    tile = jnp.concatenate(
        [positions, species.astype(f32)[None], lists, jnp.zeros((3, BLK), f32)], axis=0
    )
    near_c, near_r = square(tile, z_hi(tile))
    c4, r2 = jnp.stack([tile, *near_c]), jnp.stack([tile, near_r])
    over_x, over_y = lax.optimization_barrier((by_x(c4), by_y(r2)))
    c16 = jnp.concatenate([c4] + over_x)
    r8 = jnp.concatenate([r2] + over_y)
    place_of = jnp.stack([lax.axis_index("col"), lax.axis_index("row")])

    def info_of(tiles_c, tiles_r):
        flat = [t[:, 4, : 2 * SLOT].astype(jnp.int32).reshape(-1) for t in (tiles_c, tiles_r)]
        return jnp.concatenate([place_of] + flat)

    tab = info_of(c4, r2)
    masks = pair_mask.reshape(2, BLK, BLK)
    block = near(BLK, BLK)

    def gather_rows(v):
        four = [v] + by_x(v)
        return four, core(jnp.stack(four))

    def reduce_rows(m, name):
        m, far = lax.optimization_barrier((m, z_lo(m)))
        parts = combine_call(tab, [m, far, core(m), core(far)], into_row, name)
        return [parts[0]] + [lax.ppermute(parts[k], "col", X_SHIFT[k]) for k in (1, 2, 3)]

    m0, feat0, xm, fil1, q0, q1 = filter_call(
        tab, c16, r8, masks, embed, w_in, rbf_weight, rbf_bias, filt_weight
    )
    parts = reduce_rows(m0, "combine0")
    own_feat, sig0, mixed1 = call(
        up1_body,
        [block] * 3,
        None,
        [*parts, tile],
        [embed, w_update1, w_update2, w_in],
        name="update0",
    )
    four = [mixed1] + by_y(mixed1)
    sent = z_hi(select_call(tab, four, send_col, "select_x"))
    m1, feat1 = call(
        msg1_body, [near(2, BLK, BLK)] * 2, tab, [*four, sent], store=fil1, name="msg1"
    )
    parts = reduce_rows(m1, "combine1")
    energy, gfeat2, gmsg1 = call(
        up2_body,
        [jax.ShapeDtypeStruct((1, BLK), f32), block, block],
        None,
        [*parts, own_feat],
        [w_update1, w_update2, w_out1, w_out2[None]],
        name="update1",
    )
    tiles_c, tiles_r, gmsg1 = lax.optimization_barrier((c16, r8, gmsg1))
    tab_f = info_of(tiles_c, tiles_r)
    four, other = gather_rows(gmsg1)
    sent = z_lo(select_call(tab, [*four, other], send_row, "select_g1"))
    dfeat, grad1 = call(
        dfeat_body, [near(2, BLK, BLK)] * 2, tab, [*four, other, sent], store=fil1, name="dfeat"
    )

    def slope1(slot):
        return call(
            lambda *refs: slope1_body(*refs, slot=slot),
            [block],
            None,
            [grad1, feat1],
            store=q1,
            rows=(slot * BLK, slot * BLK + BLK // 2),
            scratch=[pltpu.VMEM((2, BLK, BLK), jnp.bfloat16), pltpu.VMEM((2, BLK, BLK), f32)],
            name=f"slope1_{slot}",
        )[0]

    far, first0 = lax.optimization_barrier((z_hi(dfeat), slope1(0)))
    parts = combine_call(tab, [dfeat, far], into_col, "combine_d")
    parts = [parts[0]] + [lax.ppermute(parts[k], "row", Y_SHIFT[k]) for k in (1, 2, 3)]
    (gmsg0,) = call(
        up3_body,
        [block],
        None,
        [*parts, gfeat2, sig0],
        [w_in, w_update1, w_update2],
        name="update2",
    )
    four, other = gather_rows(gmsg0)
    sent = z_lo(select_call(tab, [*four, other], send_row, "select_g0"))
    sent, first1 = lax.optimization_barrier((sent, slope1(1)))
    rf, cf = call(
        force_body,
        [near(2, 8, BLK)] * 2,
        tab,
        [c16, r8, xm, first0, first1, *four, other, sent],
        store=q0,
        scratch=[pltpu.VMEM((2, BLK, BLK), f32)] * 2 + [pltpu.VMEM((2, BLK, BLK), jnp.bfloat16)],
        name="force",
    )
    near_c, near_r = square(rf, z_hi(cf))
    rf8, cf4 = jnp.concatenate([rf, *near_c]), jnp.concatenate([cf, near_r])
    over_x, over_y = lax.optimization_barrier((by_x(rf8), by_y(cf4)))
    forces = sum_call(tab_f, [rf8, *over_x], [cf4, *over_y])
    return (energy.reshape(BLK), forces)


def solution(mesh):
    return jax.shard_map(
        body,
        mesh=mesh,
        in_specs=(
            P(None, ("row", "col")),
            P(("row", "col")),
            P("row", "col", None, None),
            P("row", "col", None, None, None),
            P(),
            P(),
            P(),
            P(),
            P(),
            P(),
            P(),
            P(),
            P(),
        ),
        out_specs=(P(("row", "col")), P(None, ("row", "col"))),
        check_vma=False,
    )
```
